256 devices in a mesh: ocn: 8 (over z), lon: 32 (over x, y, core).
Axes of the slice: x: 4, y: 4, z: 8, core: 2. Of those that a mesh axis runs over, the one named last changes fastest.
Arguments:
- ocean_adjoint: float32 [32, 64, 4096], P(None, 'ocn', 'lon'), may hold values from -6 to 6
- mixing_coef: float32 [31, 64, 4096], P(None, 'ocn', 'lon'), may hold values from 0.05 to 20
- land_mask: int32 [64, 4096], P('ocn', 'lon'), may hold values 0 or 1
- remap_src: int32 [8, 32, 32, 2], P('ocn', 'lon'), may hold values from 0 to 7
- remap_dst: int32 [8, 32, 32, 2], P('ocn', 'lon'), may hold values from 0 to 15
- remap_live: int32 [8, 32, 32, 2], P('ocn', 'lon'), may hold values 0 or 1
- remap_weight: bfloat16 [8, 32, 32, 2, 128, 128], P('ocn', 'lon'), may hold values from -0.5 to 0.5
- atm_u: bfloat16 [64, 64, 8192], P(None, 'ocn', 'lon'), may hold values from -6 to 6
- atm_v: bfloat16 [64, 64, 8192], P(None, 'ocn', 'lon'), may hold values from -6 to 6
- spectral_nu: float32 [64], replicated, may hold values from 0.05 to 20
- band_points: int32 [8], P('ocn'), may hold values from 1284 to 5136, as said below
Outputs:
- ocean_out: float32 [32, 64, 4096], P(None, 'ocn', 'lon')
- atm_u_out: bfloat16 [64, 64, 8192], P(None, 'ocn', 'lon')
- atm_v_out: bfloat16 [64, 64, 8192], P(None, 'ocn', 'lon')
The draws below stay inside these ranges and needn't reach their ends.
Inputs may be any that keep to these rules, and one draw needn't show every extreme that they name: `band_points`: one band has exactly 5136 points.
All inputs are finite; a program needn't handle non-finite values. No bound on the sum of `land_mask` or of `remap_live` on one device may be relied on, other than what follows from the above.
Results may differ from the reference program's by a relative error of at most 0.0059.
Values may be sent and summed in bfloat16 or wider, within the bound.
A program may use at most 256 MiB of HBM per device.

```python
import math
import jax
import jax.numpy as jnp
from jax import lax

OX = 8
OY = 128
NZ = 32
ROWS = 8
PADLON = 8192
MAXPTS = 5136
K = 1280
BLK = 128
CAP = 2
NX = 64
NY = 4096
NLAT = 64
LEV = 64
LONSEG = 256
SEG = 8
ASEG = 16
N_OCN = 8
N_LON = 32


def draw_band_points(key, part):
    first_key = jax.random.fold_in(key, 11)
    second_key = jax.random.fold_in(key, 12)
    counts = jax.random.randint(first_key, (N_OCN,), MAXPTS // 4, MAXPTS + 1)
    chosen = jax.random.randint(second_key, (), 0, N_OCN)
    return jnp.where(jnp.arange(N_OCN) == chosen, MAXPTS, counts).astype(jnp.int32)


def with_ends(result, stream_key, smallest, largest):
    shape = result.shape
    index_at = [jax.random.randint(jax.random.fold_in(stream_key, axis), (), 0, shape[axis]) for axis in range(len(shape))]
    result = result.at[tuple(index_at)].set(smallest)
    longest = shape.index(max(shape))
    index_at[longest] = (index_at[longest] + 1) % shape[longest]
    return result.at[tuple(index_at)].set(largest)


def steps_of(key, dims, split, least, top_value):
    loudness, own = 1.0, jax.random.fold_in(key, 6)
    for axis_at, blocks in split:
        draws = jnp.exp(jax.random.uniform(jax.random.fold_in(own, axis_at), (blocks,), jnp.float32, least / len(split), top_value / len(split)))
        loudness = loudness * jnp.repeat(draws, dims[axis_at] // blocks).reshape([-1 if axis == axis_at else 1 for axis in range(len(dims))])
    return loudness


def bell_draw(key, shape, width, reach, cuts=(), kind=jnp.bfloat16):
    loudness = steps_of(key, shape, cuts, -0.22, 0.18) if cuts else 1.0
    values = jax.random.normal(key, shape, jnp.float32) * width * loudness
    return jnp.minimum(jnp.maximum(values, -reach), reach).astype(kind)


def setup_inputs(seed: int = 0) -> dict:
    keys = jax.random.split(jax.random.key(seed), 12)
    ocean_adjoint = bell_draw(keys[0], (NZ, NX, NY), 1.0, 6.0, ((1, 8), (2, 32)), jnp.float32)
    mixing_coef = jnp.clip(jnp.exp(math.log(20.0) - 5.9914645 * jax.random.uniform(keys[1], (NZ - 1, NX, NY), jnp.float32) ** steps_of(keys[1], (NZ - 1, NX, NY), ((1, 8), (2, 32)), -0.2, 0.2)), 0.05, 20.0)
    land_mask = with_ends((jax.random.randint(keys[2], (NX, NY), 0, 4) < 3).astype(jnp.int32), jax.random.fold_in(keys[2], 1), 0, 1)
    remap_src = with_ends(jax.random.randint(keys[3], (N_OCN, N_LON, N_LON, CAP), 0, SEG), jax.random.fold_in(keys[3], 1), 0, SEG - 1).astype(jnp.int32)
    remap_dst = with_ends(jax.random.randint(keys[4], (N_OCN, N_LON, N_LON, CAP), 0, ASEG), jax.random.fold_in(keys[4], 1), 0, ASEG - 1).astype(jnp.int32)
    remap_live = with_ends((jax.random.randint(keys[5], (N_OCN, N_LON, N_LON, CAP), 0, 5) < 3).astype(jnp.int32), jax.random.fold_in(keys[5], 1), 0, 1)
    remap_weight = bell_draw(keys[6], (N_OCN, N_LON, N_LON, CAP, BLK, BLK), BLK ** -0.5, 0.5, ((0, 8), (1, 32)))
    atm_u = bell_draw(keys[7], (LEV, NLAT, PADLON), 1.0, 6.0, ((1, 8), (2, 32)))
    atm_v = bell_draw(keys[8], (LEV, NLAT, PADLON), 1.0, 6.0, ((1, 8), (2, 32)))
    spectral_nu = jnp.clip(jnp.exp(jax.random.uniform(keys[9], (LEV,), jnp.float32, math.log(0.05), math.log(20.0))), 0.05, 20.0)
    band_points = draw_band_points(jax.random.fold_in(keys[11], 71), 0)
    return {"ocean_adjoint": ocean_adjoint, "mixing_coef": mixing_coef, "land_mask": land_mask, "remap_src": remap_src, "remap_dst": remap_dst, "remap_live": remap_live, "remap_weight": remap_weight, "atm_u": atm_u, "atm_v": atm_v, "spectral_nu": spectral_nu, "band_points": band_points}


NU_MIX = 0.2


def tridiag_solve(coupling, forcing):
    flat_zero = jnp.zeros((1,) + forcing.shape[1:], jnp.float32)
    below = jnp.concatenate([flat_zero, coupling], 0)
    above = jnp.concatenate([coupling, flat_zero], 0)
    centre = 1.0 + below + above

    def forward(carried, inputs):
        ratio_prev, value_prev = carried
        below_level, centre_level, above_level, forcing_level = inputs
        pivot_value = centre_level + below_level * ratio_prev
        ratio_next = -above_level / pivot_value
        value_next = (forcing_level + below_level * value_prev) / pivot_value
        return (ratio_next, value_next), (ratio_next, value_next)

    ignored, (ratios, values) = lax.scan(forward, (flat_zero[0], flat_zero[0]), (below, centre, above, forcing))

    def backward(later_value, inputs):
        ratio_level, value_level = inputs
        current = value_level - ratio_level * later_value
        return current, current

    ignored, solution = lax.scan(backward, flat_zero[0], (ratios, values), reverse=True)
    return solution


def apply_stencil(padded, mask_pad):
    height = padded.shape[1] - 2
    width_cells = padded.shape[2] - 2
    centre = padded[:, 1:-1, 1:-1]
    flux_sum = jnp.zeros_like(centre)
    for offsets in ((0, 1), (2, 1), (1, 0), (1, 2)):
        row_off, col_off = offsets
        neighbour = padded[:, row_off:row_off + height, col_off:col_off + width_cells]
        neighbour_mask = mask_pad[row_off:row_off + height, col_off:col_off + width_cells]
        flux_sum = flux_sum + neighbour_mask[None] * (neighbour - centre)
    return mask_pad[1:-1, 1:-1][None] * (centre + NU_MIX * flux_sum)


def build_table(band_count, row_start, row_total):
    columns = jnp.arange(row_total, dtype=jnp.int32) + row_start
    wave_index = jnp.arange(K, dtype=jnp.int32)
    phase_index = (columns[:, None] * wave_index[None, :]) % band_count
    angles = phase_index.astype(jnp.float32) * (2.0 * math.pi) / band_count.astype(jnp.float32)
    inside = (columns < band_count).astype(jnp.float32)[:, None]
    return (jnp.concatenate([jnp.cos(angles), jnp.sin(angles)], 1) * inside).astype(jnp.bfloat16)


def finish_spectral(coeffs, viscosity, band_count, wave_table):
    wave_ratio = (jnp.arange(2 * K, dtype=jnp.int32) % K).astype(jnp.float32) / K
    damping = 1.0 / (1.0 + viscosity[:, None] * wave_ratio[None, :] * wave_ratio[None, :])
    filtered = (coeffs * damping[None, :, None, :]).astype(jnp.bfloat16)
    shape_in = filtered.shape
    grid_values = lax.dot_general(filtered.reshape(-1, shape_in[3]), wave_table, (((1,), (1,)), ((), ())), preferred_element_type=jnp.float32)
    scaled = grid_values * (2.0 / band_count.astype(jnp.float32))
    return scaled.astype(jnp.bfloat16).reshape(shape_in[0], shape_in[1], shape_in[2], wave_table.shape[0])


def reference(ocean_adjoint, mixing_coef, land_mask, remap_src, remap_dst, remap_live, remap_weight, atm_u, atm_v, spectral_nu, band_points):
    mask_float = land_mask.astype(jnp.float32)
    solved = tridiag_solve(mixing_coef, ocean_adjoint)
    padded = jnp.pad(solved, ((0, 0), (1, 1), (1, 1)))
    mask_pad = jnp.pad(mask_float, ((1, 1), (1, 1)))
    ocean_out = apply_stencil(padded, mask_pad)
    surface_flux = ocean_out[0].reshape(N_OCN, OX, N_LON, OY).transpose(0, 2, 1, 3).reshape(N_OCN, N_LON, SEG, BLK).astype(jnp.bfloat16)
    segment_ids = jnp.arange(ASEG, dtype=jnp.int32)

    def pick_rows(flux_rows, index_rows):
        return flux_rows[index_rows]

    def one_band(inputs):
        band_flux, band_src, band_dst, band_live, band_weight = inputs
        picked = jax.vmap(pick_rows)(band_flux, band_src)
        contrib = jnp.einsum("lpcab,lpcb->lpca", band_weight.astype(jnp.float32), picked.astype(jnp.float32), precision=lax.Precision.HIGHEST)
        selector = (band_dst[..., None] == segment_ids).astype(jnp.float32) * band_live.astype(jnp.float32)[..., None]
        return jnp.einsum("lpcs,lpca->psa", selector, contrib, precision=lax.Precision.HIGHEST)

    gathered = lax.map(one_band, (surface_flux, remap_src, remap_dst, remap_live, remap_weight))
    coupling = gathered.reshape(N_OCN, N_LON, ROWS, LONSEG).transpose(0, 2, 1, 3).reshape(NLAT, PADLON)
    lowest = (atm_u[LEV - 1].astype(jnp.float32) + coupling).astype(jnp.bfloat16)
    coupled_u = atm_u.at[LEV - 1].set(lowest)
    fields = jnp.stack([coupled_u, atm_v]).reshape(2, LEV, N_OCN, ROWS, PADLON).transpose(2, 0, 1, 3, 4)

    def band_spectral(inputs):
        band_fields, band_count = inputs
        wave_table = build_table(band_count, 0, PADLON)
        coeffs = jnp.dot(band_fields.reshape(-1, PADLON), wave_table, preferred_element_type=jnp.float32).reshape(2, LEV, ROWS, 2 * K)
        return finish_spectral(coeffs, spectral_nu, band_count, wave_table)

    spectral = lax.map(band_spectral, (fields, band_points))
    spectral = spectral.transpose(1, 2, 0, 3, 4).reshape(2, LEV, NLAT, PADLON)
    return ocean_out, spectral[0], spectral[1]
```

```python
import math

import jax
import jax.numpy as jnp
from jax import lax
from jax.experimental import pallas as pl
from jax.experimental.pallas import tpu as pltpu
from jax.sharding import PartitionSpec as P

K = 1280
BLK = 128
SEGLON = 256
NBLK = 21
TWROWS = 24
KT = 256
NU_MIX = 0.2

COS_C = [(-1.0) ** m * (2.0 * math.pi) ** (2 * m) / math.factorial(2 * m) for m in range(11)]
SIN_C = [(-1.0) ** m * (2.0 * math.pi) ** (2 * m + 1) / math.factorial(2 * m + 1) for m in range(11)]


def iota(shape, dim):
    return lax.broadcasted_iota(jnp.int32, shape, dim).astype(jnp.float32)


def cos_sin(steps, points):
    inverse = 1.0 / points
    turns = jnp.floor(steps * inverse + 0.5)
    part = (steps - turns * points) * inverse
    square = part * part
    cosine = jnp.full_like(square, COS_C[10])
    sine = jnp.full_like(square, SIN_C[10])
    for m in range(9, -1, -1):
        cosine = cosine * square + COS_C[m]
        sine = sine * square + SIN_C[m]
    return cosine, sine * part


def build_tables(points, coarse, fine, coarse_t, fine_t, table, table_t, twiddle):
    n_row = jnp.full((16, K), points, jnp.float32)
    step_row, wave_row = iota((16, K), 0), iota((16, K), 1)
    coarse[0], coarse[1] = cos_sin(16.0 * step_row * wave_row, n_row)
    fine[0], fine[1] = cos_sin(step_row * wave_row, n_row)
    n_tw = jnp.full((TWROWS, K), points, jnp.float32)
    twiddle[0], twiddle[1] = cos_sin(float(SEGLON) * iota((TWROWS, K), 0) * iota((TWROWS, K), 1), n_tw)
    n_t = jnp.full((K // 16, SEGLON), points, jnp.float32)
    coarse_t[0], coarse_t[1] = cos_sin(16.0 * iota((K // 16, SEGLON), 0) * iota((K // 16, SEGLON), 1), n_t)
    n_f = jnp.full((16, SEGLON), points, jnp.float32)
    fine_t[0], fine_t[1] = cos_sin(iota((16, SEGLON), 0) * iota((16, SEGLON), 1), n_f)

    def rows(p, carry):
        cos_p, sin_p = coarse[0, pl.ds(p, 1), :], coarse[1, pl.ds(p, 1), :]
        here = pl.ds(pl.multiple_of(16 * p, 16), 16)
        table[here, 0:K] = (cos_p * fine[0] - sin_p * fine[1]).astype(jnp.bfloat16)
        table[here, K : 2 * K] = (sin_p * fine[0] + cos_p * fine[1]).astype(jnp.bfloat16)
        return carry

    lax.fori_loop(0, SEGLON // 16, rows, 0)

    def rows_t(p, carry):
        cos_p, sin_p = coarse_t[0, pl.ds(p, 1), :], coarse_t[1, pl.ds(p, 1), :]
        here = pl.ds(pl.multiple_of(16 * p, 16), 16)
        table_t[0, here, :] = (cos_p * fine_t[0] - sin_p * fine_t[1]).astype(jnp.bfloat16)
        table_t[1, here, :] = (sin_p * fine_t[0] + cos_p * fine_t[1]).astype(jnp.bfloat16)
        return carry

    lax.fori_loop(0, K // 16, rows_t, 0, unroll=2)


def spectral(rows, points, damp_rows, packed, table, table_t, twiddle, raw, spread, result):
    scale = 2.0 / jnp.full((rows, KT), points, jnp.float32)

    def tile(t, carry):
        at = pl.multiple_of(t * KT, KT)
        cos_at, sin_at = pl.ds(at, KT), pl.ds(K + at, KT)
        raw[0] = jnp.dot(packed[...], table[:, cos_at], preferred_element_type=jnp.float32)
        raw[1] = jnp.dot(packed[...], table[:, sin_at], preferred_element_type=jnp.float32)
        sum_c = jnp.zeros((rows, KT), jnp.float32)
        sum_s = jnp.zeros((rows, KT), jnp.float32)
        for l in range(NBLK):
            part_c, part_s = raw[0, l * rows : (l + 1) * rows, :], raw[1, l * rows : (l + 1) * rows, :]
            tw_c, tw_s = twiddle[0, l : l + 1, cos_at], twiddle[1, l : l + 1, cos_at]
            sum_c += tw_c * part_c - tw_s * part_s
            sum_s += tw_s * part_c + tw_c * part_s
        ratio = (iota((rows, KT), 1) + (t * KT).astype(jnp.float32)) * (1.0 / K)
        damping = scale / (1.0 + damp_rows * ratio * ratio)
        sum_c *= damping
        sum_s *= damping
        for l in range(NBLK):
            tw_c, tw_s = twiddle[0, l : l + 1, cos_at], twiddle[1, l : l + 1, cos_at]
            spread[0, l * rows : (l + 1) * rows, :] = (tw_c * sum_c + tw_s * sum_s).astype(jnp.bfloat16)
            spread[1, l * rows : (l + 1) * rows, :] = (tw_c * sum_s - tw_s * sum_c).astype(jnp.bfloat16)
        k_rows = pl.ds(at, KT)
        add = jnp.dot(spread[0], table_t[0, k_rows, :], preferred_element_type=jnp.float32)
        add += jnp.dot(spread[1], table_t[1, k_rows, :], preferred_element_type=jnp.float32)

        @pl.when(t == 0)
        def _():
            result[...] = add

        @pl.when(t > 0)
        def _():
            result[...] += add

        return carry

    lax.fori_loop(0, K // KT, tile, 0)


def spectral_kernel(n_ref, nu_ref, u_ref, v_ref, out_u, out_v, coarse, fine, coarse_t, fine_t, table, table_t, twiddle, packed, raw, spread, result):
    points = n_ref[0].astype(jnp.float32)
    build_tables(points, coarse, fine, coarse_t, fine_t, table, table_t, twiddle)
    lane = iota((16, SEGLON), 1)

    def pack(l, carry):
        inside = lane + (l * SEGLON).astype(jnp.float32) < points
        for half, ref in enumerate((u_ref, v_ref)):
            block = ref[l].astype(jnp.float32).reshape(16, SEGLON)
            packed[pl.ds(pl.multiple_of(32 * l + 16 * half, 16), 16), :] = jnp.where(inside, block, 0.0).astype(jnp.bfloat16)
        return carry

    lax.fori_loop(0, NBLK, pack, 0)
    row = iota((32, KT), 0)
    odd = ((row >= 8) & (row < 16)) | (row >= 24)
    nu = jnp.where(odd, nu_ref[1], nu_ref[0])
    spectral(32, points, nu, packed, table, table_t, twiddle, raw, spread, result)

    def unpack(l, carry):
        inside = lane + (l * SEGLON).astype(jnp.float32) < points
        for half, ref in enumerate((out_u, out_v)):
            block = result[pl.ds(pl.multiple_of(32 * l + 16 * half, 16), 16), :]
            ref[l] = jnp.where(inside, block, 0.0).reshape(2, 8, SEGLON).astype(jnp.bfloat16)
        return carry

    lax.fori_loop(0, NBLK, unpack, 0)
    for l in range(NBLK, out_u.shape[0]):
        out_u[l] = jnp.zeros_like(out_u[l])
        out_v[l] = jnp.zeros_like(out_v[l])


def spectral_call(points, nu, u, v):
    m = 32 * NBLK
    vmem = pl.BlockSpec(memory_space=pltpu.VMEM)
    smem = pl.BlockSpec(memory_space=pltpu.SMEM)
    return pl.pallas_call(
        spectral_kernel,
        out_shape=(jax.ShapeDtypeStruct(u.shape, u.dtype), jax.ShapeDtypeStruct(v.shape, v.dtype)),
        in_specs=[smem, smem, vmem, vmem],
        out_specs=(vmem, vmem),
        scratch_shapes=[
            pltpu.VMEM((2, 16, K), jnp.float32),
            pltpu.VMEM((2, 16, K), jnp.float32),
            pltpu.VMEM((2, K // 16, SEGLON), jnp.float32),
            pltpu.VMEM((2, 16, SEGLON), jnp.float32),
            pltpu.VMEM((SEGLON, 2 * K), jnp.bfloat16),
            pltpu.VMEM((2, K, SEGLON), jnp.bfloat16),
            pltpu.VMEM((2, TWROWS, K), jnp.float32),
            pltpu.VMEM((m, SEGLON), jnp.bfloat16),
            pltpu.VMEM((2, m, KT), jnp.float32),
            pltpu.VMEM((2, m, KT), jnp.bfloat16),
            pltpu.VMEM((m, SEGLON), jnp.float32),
        ],
        compiler_params=pltpu.CompilerParams(vmem_limit_bytes=40 << 20),
        name="spectral",
    )(points, nu, u, v)


def solve_kernel(mix_ref, force_ref, out_ref, ratio):
    levels = force_ref.shape[0]
    zero = jnp.zeros(force_ref.shape[1:], jnp.float32)
    rat, val, below = zero, zero, zero
    for z in range(levels - 1, -1, -1):
        above = mix_ref[z - 1] if z > 0 else zero
        inv = 1.0 / (1.0 + above + below * (1.0 - rat))
        val = (force_ref[z] + below * val) * inv
        rat = above * inv
        out_ref[z] = val
        ratio[z] = rat
        below = above
    s = out_ref[0]
    for z in range(1, levels):
        s = out_ref[z] + ratio[z] * s
        out_ref[z] = s


def solve(mix, force):
    vmem = pl.BlockSpec(memory_space=pltpu.VMEM)
    return pl.pallas_call(
        solve_kernel,
        out_shape=jax.ShapeDtypeStruct(force.shape, jnp.float32),
        in_specs=[vmem, vmem],
        out_specs=vmem,
        scratch_shapes=[pltpu.VMEM(force.shape, jnp.float32)],
        name="solve",
    )(mix, force)


def remap_kernel(src_ref, flux_ref, weight_ref, out_ref):
    def owner(p, carry):
        zero = jnp.zeros((6, BLK), jnp.float32)
        one = flux_ref[pl.ds(src_ref[2 * p], 1), :]
        two = flux_ref[pl.ds(src_ref[2 * p + 1], 1), :]
        blank = jnp.zeros((1, BLK), jnp.float32)
        left = jnp.concatenate([jnp.concatenate([one, blank], 1), jnp.concatenate([blank, two], 1)], 0)
        lhs = jnp.concatenate([left, jnp.concatenate([zero, zero], 1)], 0).astype(jnp.bfloat16)
        both = jnp.concatenate([weight_ref[p, 0], weight_ref[p, 1]], 1)
        got = lax.dot_general(lhs, both, (((1,), (1,)), ((), ())), preferred_element_type=jnp.float32)
        out_ref[p] = got[0:2]
        return carry

    lax.fori_loop(0, weight_ref.shape[0], owner, 0)


def remap(src, flux, weights):
    vmem = pl.BlockSpec(memory_space=pltpu.VMEM)
    smem = pl.BlockSpec(memory_space=pltpu.SMEM)
    return pl.pallas_call(
        remap_kernel,
        out_shape=jax.ShapeDtypeStruct((weights.shape[0], 2, BLK), jnp.float32),
        in_specs=[smem, vmem, vmem],
        out_specs=vmem,
        compiler_params=pltpu.CompilerParams(vmem_limit_bytes=20 << 20),
        name="remap",
    )(src, flux, weights)


def with_halo(cells, sides, width):
    for axis, dim in sides:
        count = lax.axis_size(axis)
        ends = count - 1
        head = lax.slice_in_dim(cells, 0, width, axis=dim)
        tail = lax.slice_in_dim(cells, cells.shape[dim] - width, cells.shape[dim], axis=dim)
        cells = jnp.concatenate(
            [
                lax.ppermute(tail, axis, [(i, (i + 1) % count) for i in range(ends)]),
                cells,
                lax.ppermute(head, axis, [((i + 1) % count, i) for i in range(ends)]),
            ],
            axis=dim,
        )
    return cells


def apply_stencil(padded, mask_pad):
    height = padded.shape[1] - 2
    width_cells = padded.shape[2] - 2
    centre = padded[:, 1:-1, 1:-1]
    flux_sum = jnp.zeros_like(centre)
    for offsets in ((0, 1), (2, 1), (1, 0), (1, 2)):
        row_off, col_off = offsets
        neighbour = padded[:, row_off : row_off + height, col_off : col_off + width_cells]
        neighbour_mask = mask_pad[row_off : row_off + height, col_off : col_off + width_cells]
        flux_sum = flux_sum + neighbour_mask[None] * (neighbour - centre)
    return mask_pad[1:-1, 1:-1][None] * (centre + NU_MIX * flux_sum)


def per_device(
    ocean_adjoint,
    mixing_coef,
    land_mask,
    remap_src,
    remap_dst,
    remap_live,
    remap_weight,
    atm_u,
    atm_v,
    spectral_nu,
    band_points,
):
    lon_devices = lax.axis_size("lon")
    levels, band_rows, lon_points = atm_u.shape
    share = levels // lon_devices
    swap = lambda x: lax.all_to_all(x, "lon", split_axis=0, concat_axis=0, tiled=True)
    piece_v = swap(atm_v.reshape(lon_devices, share, band_rows, lon_points))
    mask_float = land_mask.astype(jnp.float32)
    solved = solve(mixing_coef, ocean_adjoint)
    stacked = jnp.concatenate([solved, mask_float[None]], 0)
    extended = with_halo(stacked, (("ocn", 1), ("lon", 2)), 1)
    ocean_depth = solved.shape[0]
    ocean_out = apply_stencil(extended[:ocean_depth], extended[ocean_depth])
    slot_count = remap_src.shape[3]
    weights = remap_weight.reshape(lon_devices, slot_count, BLK, BLK)
    flux = ocean_out[0].astype(jnp.bfloat16).astype(jnp.float32)
    contrib = remap(remap_src.reshape(-1), flux, weights)
    live = remap_live.reshape(lon_devices, slot_count)
    contrib = contrib * live.astype(jnp.float32)[:, :, None]
    code = jnp.where(live == 1, remap_dst.reshape(lon_devices, slot_count), -1).astype(jnp.float32)
    codes = jnp.broadcast_to(code[:, :, None], contrib.shape)
    both = swap(jnp.concatenate([contrib, codes], 1))
    received, dest = both[:, :slot_count], both[:, slot_count:, 0]
    segments = band_rows * lon_points // BLK
    selector = (dest[:, :, None] == jnp.arange(segments).astype(jnp.float32)).astype(jnp.float32)
    surface = jnp.einsum("pcs,pca->sa", selector, received, precision=lax.Precision.HIGHEST)
    lowest = (atm_u[levels - 1].astype(jnp.float32) + surface.reshape(band_rows, lon_points)).astype(jnp.bfloat16)
    coupled_u = jnp.concatenate([atm_u[: levels - 1], lowest[None]], 0)
    piece_u = swap(coupled_u.reshape(lon_devices, share, band_rows, lon_points))
    nu = lax.dynamic_slice_in_dim(spectral_nu, lax.axis_index("lon") * share, share, 0)
    new_u, new_v = spectral_call(band_points, nu, piece_u, piece_v)
    return (ocean_out, swap(new_u).reshape(atm_u.shape), swap(new_v).reshape(atm_v.shape))


def solution(mesh):
    placed = (
        P(None, "ocn", "lon"),
        P(None, "ocn", "lon"),
        P("ocn", "lon"),
        P("ocn", "lon", None, None),
        P("ocn", "lon", None, None),
        P("ocn", "lon", None, None),
        P("ocn", "lon", None, None, None, None),
        P(None, "ocn", "lon"),
        P(None, "ocn", "lon"),
        P(),
        P("ocn"),
    )
    return jax.shard_map(
        per_device,
        mesh=mesh,
        in_specs=placed,
        out_specs=(P(None, "ocn", "lon"), P(None, "ocn", "lon"), P(None, "ocn", "lon")),
        check_vma=False,
    )
```

```python
import math

import jax
import jax.numpy as jnp
from jax import lax
from jax.experimental import pallas as pl
from jax.experimental.pallas import tpu as pltpu
from jax.sharding import PartitionSpec as P

K = 1280
BLK = 128
SEGLON = 256
NBLK = 21
TWROWS = 24
KT = 256
NU_MIX = 0.2
MESH = pl.DeviceIdType.MESH

COS_C = [(-1.0) ** m * (2.0 * math.pi) ** (2 * m) / math.factorial(2 * m) for m in range(11)]
SIN_C = [(-1.0) ** m * (2.0 * math.pi) ** (2 * m + 1) / math.factorial(2 * m + 1) for m in range(11)]


def iota(shape, dim):
    return lax.broadcasted_iota(jnp.int32, shape, dim).astype(jnp.float32)


def cos_sin(steps, points):
    inverse = 1.0 / points
    turns = jnp.floor(steps * inverse + 0.5)
    part = (steps - turns * points) * inverse
    square = part * part
    cosine = jnp.full_like(square, COS_C[10])
    sine = jnp.full_like(square, SIN_C[10])
    for m in range(9, -1, -1):
        cosine = cosine * square + COS_C[m]
        sine = sine * square + SIN_C[m]
    return cosine, sine * part


def build_tables(points, coarse, fine, coarse_t, fine_t, table, table_t, twiddle):
    n_row = jnp.full((16, K), points, jnp.float32)
    step_row, wave_row = iota((16, K), 0), iota((16, K), 1)
    coarse[0], coarse[1] = cos_sin(16.0 * step_row * wave_row, n_row)
    fine[0], fine[1] = cos_sin(step_row * wave_row, n_row)
    n_tw = jnp.full((TWROWS, K), points, jnp.float32)
    twiddle[0], twiddle[1] = cos_sin(float(SEGLON) * iota((TWROWS, K), 0) * iota((TWROWS, K), 1), n_tw)
    n_t = jnp.full((K // 16, SEGLON), points, jnp.float32)
    coarse_t[0], coarse_t[1] = cos_sin(16.0 * iota((K // 16, SEGLON), 0) * iota((K // 16, SEGLON), 1), n_t)
    n_f = jnp.full((16, SEGLON), points, jnp.float32)
    fine_t[0], fine_t[1] = cos_sin(iota((16, SEGLON), 0) * iota((16, SEGLON), 1), n_f)

    def rows(p, carry):
        cos_p, sin_p = coarse[0, pl.ds(p, 1), :], coarse[1, pl.ds(p, 1), :]
        here = pl.ds(pl.multiple_of(16 * p, 16), 16)
        table[here, 0:K] = (cos_p * fine[0] - sin_p * fine[1]).astype(jnp.bfloat16)
        table[here, K : 2 * K] = (sin_p * fine[0] + cos_p * fine[1]).astype(jnp.bfloat16)
        return carry

    lax.fori_loop(0, SEGLON // 16, rows, 0)

    def rows_t(p, carry):
        cos_p, sin_p = coarse_t[0, pl.ds(p, 1), :], coarse_t[1, pl.ds(p, 1), :]
        here = pl.ds(pl.multiple_of(16 * p, 16), 16)
        table_t[0, here, :] = (cos_p * fine_t[0] - sin_p * fine_t[1]).astype(jnp.bfloat16)
        table_t[1, here, :] = (sin_p * fine_t[0] + cos_p * fine_t[1]).astype(jnp.bfloat16)
        return carry

    lax.fori_loop(0, K // 16, rows_t, 0, unroll=2)


def spectral(rows, points, damp_rows, packed, table, table_t, twiddle, raw, spread, result):
    scale = 2.0 / jnp.full((rows, KT), points, jnp.float32)

    def tile(t, carry):
        at = pl.multiple_of(t * KT, KT)
        cos_at, sin_at = pl.ds(at, KT), pl.ds(K + at, KT)
        raw[0] = jnp.dot(packed[...], table[:, cos_at], preferred_element_type=jnp.float32)
        raw[1] = jnp.dot(packed[...], table[:, sin_at], preferred_element_type=jnp.float32)
        sum_c = jnp.zeros((rows, KT), jnp.float32)
        sum_s = jnp.zeros((rows, KT), jnp.float32)
        for l in range(NBLK):
            part_c, part_s = raw[0, l * rows : (l + 1) * rows, :], raw[1, l * rows : (l + 1) * rows, :]
            tw_c, tw_s = twiddle[0, l : l + 1, cos_at], twiddle[1, l : l + 1, cos_at]
            sum_c += tw_c * part_c - tw_s * part_s
            sum_s += tw_s * part_c + tw_c * part_s
        ratio = (iota((rows, KT), 1) + (t * KT).astype(jnp.float32)) * (1.0 / K)
        damping = scale / (1.0 + damp_rows * ratio * ratio)
        sum_c *= damping
        sum_s *= damping
        for l in range(NBLK):
            tw_c, tw_s = twiddle[0, l : l + 1, cos_at], twiddle[1, l : l + 1, cos_at]
            spread[0, l * rows : (l + 1) * rows, :] = (tw_c * sum_c + tw_s * sum_s).astype(jnp.bfloat16)
            spread[1, l * rows : (l + 1) * rows, :] = (tw_c * sum_s - tw_s * sum_c).astype(jnp.bfloat16)
        k_rows = pl.ds(at, KT)
        add = jnp.dot(spread[0], table_t[0, k_rows, :], preferred_element_type=jnp.float32)
        add += jnp.dot(spread[1], table_t[1, k_rows, :], preferred_element_type=jnp.float32)

        @pl.when(t == 0)
        def _():
            result[...] = add

        @pl.when(t > 0)
        def _():
            result[...] += add

        return carry

    lax.fori_loop(0, K // KT, tile, 0)


def shift_rows(cells, down, edge):
    row = lax.broadcasted_iota(jnp.int32, cells.shape, 0)
    last = cells.shape[0] - 1
    if down:
        return jnp.where(row == 0, edge, pltpu.roll(cells, 1, 0))
    return jnp.where(row == last, edge, pltpu.roll(cells, last, 0))


def shift_cols(cells, right, edge):
    lane = lax.broadcasted_iota(jnp.int32, cells.shape, 1)
    last = cells.shape[1] - 1
    if right:
        return jnp.where(lane == 0, edge, pltpu.roll(cells, 1, 1))
    return jnp.where(lane == last, edge, pltpu.roll(cells, last, 1))


def window_kernel(
    n_ref, nu_ref, src_ref, dst_ref, live_ref, force_hbm, mix_hbm, mask_hbm, weight_hbm, u_hbm, v_hbm,
    out_ocean, out_u, out_v,
    force, mix, mask, weight, last_u, load_sem,
    cells, ratio, ocean, send_n, send_s, send_w, send_e, got_n, got_s, got_w, got_e, halo_send, halo_recv,
    flux, note, notes, note_send, note_recv,
    stage, got_u, got_v, fwd_send, fwd_recv,
    coarse, fine, coarse_t, fine_t, table, table_t, twiddle,
    packed, raw, spread, result, back_u, back_v, blank, back_send, back_recv, ocean_sem,
):
    me, oc = lax.axis_index("lon"), lax.axis_index("ocn")
    n_lon, n_ocn = lax.axis_size("lon"), lax.axis_size("ocn")
    levels = cells.shape[0] - 1
    last_owner = n_lon - 1
    share = 2
    source = me < NBLK

    def mine(t):
        return pl.ds(share * t, share)

    loads = [
        pltpu.make_async_copy(force_hbm, force, load_sem.at[0]),
        pltpu.make_async_copy(mix_hbm, mix, load_sem.at[1]),
        pltpu.make_async_copy(mask_hbm, mask, load_sem.at[2]),
        pltpu.make_async_copy(weight_hbm.at[pl.ds(0, NBLK)], weight, load_sem.at[3]),
        pltpu.make_async_copy(u_hbm.at[mine(last_owner)], last_u, load_sem.at[4]),
    ]
    for load in loads:
        load.start()

    barrier = pltpu.get_barrier_semaphore()

    def greet(i, carry):
        pl.semaphore_signal(barrier, inc=1, device_id={"lon": lax.rem(me + i, n_lon)}, device_id_type=MESH)
        return carry

    lax.fori_loop(1, n_lon, greet, 0)

    @pl.when(oc > 0)
    def _():
        pl.semaphore_signal(barrier, inc=1, device_id={"ocn": oc - 1}, device_id_type=MESH)

    @pl.when(oc < n_ocn - 1)
    def _():
        pl.semaphore_signal(barrier, inc=1, device_id={"ocn": oc + 1}, device_id_type=MESH)

    for load in loads[:3]:
        load.wait()
    zero = jnp.zeros(force.shape[1:], jnp.float32)
    rat, val, below = zero, zero, zero
    for z in range(levels - 1, -1, -1):
        above = mix[z - 1] if z > 0 else zero
        inv = 1.0 / (1.0 + above + below * (1.0 - rat))
        val = (force[z] + below * val) * inv
        rat = above * inv
        cells[z] = val
        ratio[z] = rat
        below = above
    lane = lax.broadcasted_iota(jnp.int32, zero.shape, 1)
    west, east = zero, zero
    send_n[pl.ds(levels, 8), :] = zero
    send_s[pl.ds(levels, 8), :] = zero
    s = zero
    for z in range(levels + 1):
        if z < levels:
            s = cells[z] + ratio[z] * s if z > 0 else cells[0]
        else:
            s = mask[...].astype(jnp.float32)
        cells[z] = s
        send_n[z : z + 1, :] = s[0:1, :]
        send_s[z : z + 1, :] = s[7:8, :]
        west = jnp.where(lane == z, jnp.broadcast_to(s[:, 0:1], s.shape), west)
        east = jnp.where(lane == z, jnp.broadcast_to(s[:, BLK - 1 : BLK], s.shape), east)
    send_w[...] = west
    send_e[...] = east

    pl.semaphore_wait(barrier, n_lon - 1 + (oc > 0).astype(jnp.int32) + (oc < n_ocn - 1).astype(jnp.int32))

    sides = (
        (oc > 0, oc < n_ocn - 1, {"ocn": oc - 1}, send_n, got_s),
        (oc < n_ocn - 1, oc > 0, {"ocn": oc + 1}, send_s, got_n),
        (me > 0, me < n_lon - 1, {"lon": me - 1}, send_w, got_e),
        (me < n_lon - 1, me > 0, {"lon": me + 1}, send_e, got_w),
    )

    def halo(i):
        has, gets, where, out, into = sides[i]
        return has, gets, into, pltpu.make_async_remote_copy(
            src_ref=out, dst_ref=into, send_sem=halo_send.at[i], recv_sem=halo_recv.at[i], device_id=where, device_id_type=MESH
        )

    for i in range(4):
        has, gets, into, copy = halo(i)
        pl.when(has)(copy.start)

        @pl.when(jnp.logical_not(gets))
        def _(into=into):
            into[...] = jnp.zeros_like(into)

    def forward(i, carry):
        t = lax.rem(me + i, n_lon)
        pltpu.make_async_remote_copy(
            src_ref=v_hbm.at[mine(t)], dst_ref=got_v.at[me], send_sem=fwd_send.at[0], recv_sem=fwd_recv.at[0], device_id={"lon": t}, device_id_type=MESH
        ).start()

        @pl.when(t != last_owner)
        def _():
            pltpu.make_async_remote_copy(
                src_ref=u_hbm.at[mine(t)], dst_ref=got_u.at[me], send_sem=fwd_send.at[1], recv_sem=fwd_recv.at[1], device_id={"lon": t}, device_id_type=MESH
            ).start()

        return carry

    @pl.when(source)
    def _():
        lax.fori_loop(1, n_lon, forward, 0)
        pltpu.make_async_copy(v_hbm.at[mine(me)], got_v.at[me], fwd_recv.at[0]).start()
        pltpu.make_async_copy(u_hbm.at[mine(me)], got_u.at[me], fwd_recv.at[1]).start()

    points = n_ref[0].astype(jnp.float32)
    build_tables(points, coarse, fine, coarse_t, fine_t, table, table_t, twiddle)

    for i in range(4):
        has, gets, into, copy = halo(i)
        pl.when(gets)(copy.wait_recv)
        pl.when(has)(copy.wait_send)

    m = cells[levels]
    m_n, m_s = shift_rows(m, True, got_n[levels : levels + 1, :]), shift_rows(m, False, got_s[levels : levels + 1, :])
    m_w = shift_cols(m, True, jnp.broadcast_to(got_w[:, levels : levels + 1], m.shape))
    m_e = shift_cols(m, False, jnp.broadcast_to(got_e[:, levels : levels + 1], m.shape))

    def mixed(z):
        s = cells[z]
        near = m_n * (shift_rows(s, True, got_n[z : z + 1, :]) - s)
        near += m_s * (shift_rows(s, False, got_s[z : z + 1, :]) - s)
        near += m_w * (shift_cols(s, True, jnp.broadcast_to(got_w[:, z : z + 1], s.shape)) - s)
        near += m_e * (shift_cols(s, False, jnp.broadcast_to(got_e[:, z : z + 1], s.shape)) - s)
        return m * (s + NU_MIX * near)

    surface = mixed(0)
    ocean[0] = surface
    flux[...] = surface.astype(jnp.bfloat16).astype(jnp.float32)
    loads[3].wait()

    def owner(p, carry):
        one = flux[pl.ds(src_ref[p, 0], 1), :]
        two = flux[pl.ds(src_ref[p, 1], 1), :]
        row = lax.broadcasted_iota(jnp.int32, (8, BLK), 0)
        lhs = jnp.concatenate([jnp.where(row == 0, one, 0.0), jnp.where(row == 1, two, 0.0)], 1).astype(jnp.bfloat16)
        both = jnp.concatenate([weight[p, 0], weight[p, 1]], 1)
        got = lax.dot_general(lhs, both, (((1,), (1,)), ((), ())), preferred_element_type=jnp.float32)
        code_0 = live_ref[p, 0] * (dst_ref[p, 0] + 1) - 1
        code_1 = live_ref[p, 1] * (dst_ref[p, 1] + 1) - 1
        codes = jnp.where(row == 2, code_0, code_1).astype(jnp.float32)
        note[p] = jnp.where(row < 2, got, codes)[0:4]
        return carry

    lax.fori_loop(0, NBLK, owner, 0, unroll=3)

    def tell(p, carry):
        @pl.when(p != me)
        def _():
            pltpu.make_async_remote_copy(
                src_ref=note.at[p], dst_ref=notes.at[me], send_sem=note_send, recv_sem=note_recv, device_id={"lon": p}, device_id_type=MESH
            ).start()

        return carry

    lax.fori_loop(0, NBLK, tell, 0)

    @pl.when(source)
    def _():
        pltpu.make_async_copy(note.at[me], notes.at[me], note_recv).start()

    for z in range(1, levels):
        ocean[z] = mixed(z)
    ocean_copy = pltpu.make_async_copy(ocean, out_ocean, ocean_sem)
    ocean_copy.start()
    loads[4].wait()

    @pl.when(source)
    def _():
        pltpu.make_async_copy(notes, notes, note_recv).wait()
        even = 2.0 * iota((8, BLK), 0)
        odd = even + 1.0

        def add(l, sums):
            sum_even, sum_odd = sums
            block = notes[l]
            for c in range(2):
                value, code = block[c : c + 1, :], block[c + 2 : c + 3, :]
                sum_even += jnp.where(code == even, value, 0.0)
                sum_odd += jnp.where(code == odd, value, 0.0)
            return sum_even, sum_odd

        blank_sum = jnp.zeros((8, BLK), jnp.float32)
        sum_even, sum_odd = lax.fori_loop(0, n_lon, add, (blank_sum, blank_sum), unroll=4)
        coupling = jnp.concatenate([sum_even, sum_odd], 1)
        stage[0] = last_u[0]
        stage[1] = (last_u[1].astype(jnp.float32) + coupling).astype(jnp.bfloat16)
        pltpu.make_async_remote_copy(
            src_ref=stage, dst_ref=got_u.at[me], send_sem=fwd_send.at[1], recv_sem=fwd_recv.at[1], device_id={"lon": last_owner}, device_id_type=MESH
        ).start()

    column = iota((16, SEGLON), 1)
    row = iota((16, KT), 0)
    nu = jnp.where(row < 8, nu_ref[share * me], nu_ref[share * me + 1])
    for f, (got, back, out) in enumerate(((got_v, back_v, out_v), (got_u, back_u, out_u))):
        pltpu.make_async_copy(got, got, fwd_recv.at[f]).wait()

        def pack(l, carry, got=got):
            inside = column + (l * SEGLON).astype(jnp.float32) < points
            block = got[l].astype(jnp.float32).reshape(16, SEGLON)
            packed[pl.ds(pl.multiple_of(16 * l, 16), 16), :] = jnp.where(inside, block, 0.0).astype(jnp.bfloat16)
            return carry

        lax.fori_loop(0, NBLK, pack, 0)
        spectral(16, points, nu, packed, table, table_t, twiddle, raw, spread, result)

        def unpack(l, carry, back=back, out=out, f=f):
            inside = column + (l * SEGLON).astype(jnp.float32) < points
            block = result[pl.ds(pl.multiple_of(16 * l, 16), 16), :]
            back[l] = jnp.where(inside, block, 0.0).reshape(2, 8, SEGLON).astype(jnp.bfloat16)

            @pl.when(l != me)
            def _():
                pltpu.make_async_remote_copy(
                    src_ref=back.at[l], dst_ref=out.at[mine(me)], send_sem=back_send.at[f], recv_sem=back_recv.at[f], device_id={"lon": l}, device_id_type=MESH
                ).start()

            return carry

        lax.fori_loop(0, NBLK, unpack, 0)

        @pl.when(source)
        def _(back=back, out=out, f=f):
            pltpu.make_async_copy(back.at[me], out.at[mine(me)], back_recv.at[f]).start()

        @pl.when(jnp.logical_not(source))
        def _(back=back, out=out, f=f):
            if f == 0:
                blank[...] = jnp.zeros_like(blank)
            pltpu.make_async_copy(blank, out, back_recv.at[f]).start()

    ocean_copy.wait()

    @pl.when(source)
    def _():
        for f in range(2):
            sent = v_hbm.at[pl.ds(0, share * (n_lon - 1))]
            pltpu.make_async_copy(sent, sent, fwd_send.at[f]).wait()
        told = note.at[pl.ds(0, NBLK - 1)]
        pltpu.make_async_copy(told, told, note_send).wait()

    @pl.when(jnp.logical_not(source))
    def _():
        pltpu.make_async_copy(note, note, note_send).wait()

    for f, (back, out) in enumerate(((back_v, out_v), (back_u, out_u))):

        @pl.when(source)
        def _(back=back, f=f):
            sent = back.at[pl.ds(0, NBLK - 1)]
            pltpu.make_async_copy(sent, sent, back_send.at[f]).wait()

        @pl.when(jnp.logical_not(source))
        def _(back=back, f=f):
            pltpu.make_async_copy(back, back, back_send.at[f]).wait()

        pltpu.make_async_copy(out, out, back_recv.at[f]).wait()


def per_device(
    ocean_adjoint,
    mixing_coef,
    land_mask,
    remap_src,
    remap_dst,
    remap_live,
    remap_weight,
    atm_u,
    atm_v,
    spectral_nu,
    band_points,
):
    lon_devices = lax.axis_size("lon")
    levels = ocean_adjoint.shape[0]
    slots = remap_src.shape[2:]
    tile = ocean_adjoint.shape[1:]
    m = 16 * NBLK
    f32, bf16, dma = jnp.float32, jnp.bfloat16, pltpu.SemaphoreType.DMA
    smem = pl.BlockSpec(memory_space=pltpu.SMEM)
    hbm = pl.BlockSpec(memory_space=pl.ANY)
    two = (2,) + atm_u.shape[1:]
    edge = (levels + 8, BLK)
    return pl.pallas_call(
        window_kernel,
        out_shape=(
            jax.ShapeDtypeStruct(ocean_adjoint.shape, f32),
            jax.ShapeDtypeStruct(atm_u.shape, bf16),
            jax.ShapeDtypeStruct(atm_v.shape, bf16),
        ),
        in_specs=[smem] * 5 + [hbm] * 6,
        out_specs=(hbm, hbm, hbm),
        scratch_shapes=[
            pltpu.VMEM(ocean_adjoint.shape, f32),
            pltpu.VMEM(mixing_coef.shape, f32),
            pltpu.VMEM(land_mask.shape, jnp.int32),
            pltpu.VMEM((NBLK, slots[1], BLK, BLK), bf16),
            pltpu.VMEM(two, bf16),
            dma((5,)),
            pltpu.VMEM((levels + 1,) + tile, f32),
            pltpu.VMEM((levels,) + tile, f32),
            pltpu.VMEM((levels,) + tile, f32),
            pltpu.VMEM(edge, f32),
            pltpu.VMEM(edge, f32),
            pltpu.VMEM(tile, f32),
            pltpu.VMEM(tile, f32),
            pltpu.VMEM(edge, f32),
            pltpu.VMEM(edge, f32),
            pltpu.VMEM(tile, f32),
            pltpu.VMEM(tile, f32),
            dma((4,)),
            dma((4,)),
            pltpu.VMEM(tile, f32),
            pltpu.VMEM((NBLK, 4, BLK), f32),
            pltpu.VMEM((lon_devices, 4, BLK), f32),
            dma,
            dma,
            pltpu.VMEM(two, bf16),
            pltpu.VMEM((NBLK,) + two, bf16),
            pltpu.VMEM((NBLK,) + two, bf16),
            dma((2,)),
            dma((2,)),
            pltpu.VMEM((2, 16, K), f32),
            pltpu.VMEM((2, 16, K), f32),
            pltpu.VMEM((2, K // 16, SEGLON), f32),
            pltpu.VMEM((2, 16, SEGLON), f32),
            pltpu.VMEM((SEGLON, 2 * K), bf16),
            pltpu.VMEM((2, K, SEGLON), bf16),
            pltpu.VMEM((2, TWROWS, K), f32),
            pltpu.VMEM((m, SEGLON), bf16),
            pltpu.VMEM((2, m, KT), f32),
            pltpu.VMEM((2, m, KT), bf16),
            pltpu.VMEM((m, SEGLON), f32),
            pltpu.VMEM((NBLK,) + two, bf16),
            pltpu.VMEM((NBLK,) + two, bf16),
            pltpu.VMEM(atm_u.shape, bf16),
            dma((2,)),
            dma((2,)),
            dma,
        ],
        compiler_params=pltpu.CompilerParams(collective_id=0, has_side_effects=True, vmem_limit_bytes=48 << 20),
        name="window",
    )(
        band_points,
        spectral_nu,
        remap_src.reshape(slots),
        remap_dst.reshape(slots),
        remap_live.reshape(slots),
        ocean_adjoint,
        mixing_coef,
        land_mask,
        remap_weight.reshape(remap_weight.shape[2:]),
        atm_u,
        atm_v,
    )


def solution(mesh):
    placed = (
        P(None, "ocn", "lon"),
        P(None, "ocn", "lon"),
        P("ocn", "lon"),
        P("ocn", "lon", None, None),
        P("ocn", "lon", None, None),
        P("ocn", "lon", None, None),
        P("ocn", "lon", None, None, None, None),
        P(None, "ocn", "lon"),
        P(None, "ocn", "lon"),
        P(),
        P("ocn"),
    )
    return jax.shard_map(
        per_device,
        mesh=mesh,
        in_specs=placed,
        out_specs=(P(None, "ocn", "lon"), P(None, "ocn", "lon"), P(None, "ocn", "lon")),
        check_vma=False,
    )
```

```python
import math

import jax
import jax.numpy as jnp
from jax import lax
from jax.experimental import pallas as pl
from jax.experimental.pallas import tpu as pltpu
from jax.sharding import PartitionSpec as P

K = 1280
BLK = 128
SEGLON = 256
NBLK = 21
TWROWS = 24
KT = 256
NU_MIX = 0.2
MESH = pl.DeviceIdType.MESH

COS_C = [(-1.0) ** m * (2.0 * math.pi) ** (2 * m) / math.factorial(2 * m) for m in range(11)]
SIN_C = [(-1.0) ** m * (2.0 * math.pi) ** (2 * m + 1) / math.factorial(2 * m + 1) for m in range(11)]


def iota(shape, dim):
    return lax.broadcasted_iota(jnp.int32, shape, dim).astype(jnp.float32)


def cos_sin(steps, points):
    inverse = 1.0 / points
    turns = jnp.floor(steps * inverse + 0.5)
    part = (steps - turns * points) * inverse
    square = part * part
    cosine = jnp.full_like(square, COS_C[10])
    sine = jnp.full_like(square, SIN_C[10])
    for m in range(9, -1, -1):
        cosine = cosine * square + COS_C[m]
        sine = sine * square + SIN_C[m]
    return cosine, sine * part


def build_tables(points, coarse, fine, coarse_t, fine_t, table, table_t, twiddle):
    n_row = jnp.full((16, K), points, jnp.float32)
    step_row, wave_row = iota((16, K), 0), iota((16, K), 1)
    coarse[0], coarse[1] = cos_sin(16.0 * step_row * wave_row, n_row)
    fine[0], fine[1] = cos_sin(step_row * wave_row, n_row)
    n_tw = jnp.full((TWROWS, K), points, jnp.float32)
    twiddle[0], twiddle[1] = cos_sin(float(SEGLON) * iota((TWROWS, K), 0) * iota((TWROWS, K), 1), n_tw)
    n_t = jnp.full((K // 16, SEGLON), points, jnp.float32)
    coarse_t[0], coarse_t[1] = cos_sin(16.0 * iota((K // 16, SEGLON), 0) * iota((K // 16, SEGLON), 1), n_t)
    n_f = jnp.full((16, SEGLON), points, jnp.float32)
    fine_t[0], fine_t[1] = cos_sin(iota((16, SEGLON), 0) * iota((16, SEGLON), 1), n_f)

    def rows(p, carry):
        cos_p, sin_p = coarse[0, pl.ds(p, 1), :], coarse[1, pl.ds(p, 1), :]
        here = pl.ds(pl.multiple_of(16 * p, 16), 16)
        table[here, 0:K] = (cos_p * fine[0] - sin_p * fine[1]).astype(jnp.bfloat16)
        table[here, K : 2 * K] = (sin_p * fine[0] + cos_p * fine[1]).astype(jnp.bfloat16)
        return carry

    lax.fori_loop(0, SEGLON // 16, rows, 0)

    def rows_t(p, carry):
        cos_p, sin_p = coarse_t[0, pl.ds(p, 1), :], coarse_t[1, pl.ds(p, 1), :]
        here = pl.ds(pl.multiple_of(16 * p, 16), 16)
        table_t[here, :] = (cos_p * fine_t[0] - sin_p * fine_t[1]).astype(jnp.bfloat16)
        table_t[pl.ds(pl.multiple_of(K + 16 * p, 16), 16), :] = (sin_p * fine_t[0] + cos_p * fine_t[1]).astype(jnp.bfloat16)
        return carry

    lax.fori_loop(0, K // 16, rows_t, 0, unroll=2)


def spectral(rows, points, viscosity, packed, table, table_t, twiddle, raw, spread, result):
    total = NBLK * rows
    half = (total // 2 + 15) // 16 * 16
    scale = 2.0 / jnp.full((rows, KT), points, jnp.float32)

    def transform(t):
        for part in range(2):
            at = part * K + t * KT
            raw[t, part] = jnp.dot(packed[...], table[:, at : at + KT], preferred_element_type=jnp.float32)

    def twist(t):
        cos_at, sin_at = slice(t * KT, (t + 1) * KT), slice(K + t * KT, K + (t + 1) * KT)
        sum_c = jnp.zeros((rows, KT), jnp.float32)
        sum_s = jnp.zeros((rows, KT), jnp.float32)
        for l in range(NBLK):
            here = slice(l * rows, (l + 1) * rows)
            part_c, part_s = raw[t, 0, here, :], raw[t, 1, here, :]
            tw_c, tw_s = twiddle[0, l : l + 1, cos_at], twiddle[1, l : l + 1, cos_at]
            sum_c += tw_c * part_c - tw_s * part_s
            sum_s += tw_s * part_c + tw_c * part_s
        ratio = (iota((rows, KT), 1) + float(t * KT)) * (1.0 / K)
        damping = scale / (1.0 + viscosity * ratio * ratio)
        sum_c *= damping
        sum_s *= damping
        for l in range(NBLK):
            here = slice(l * rows, (l + 1) * rows)
            tw_c, tw_s = twiddle[0, l : l + 1, cos_at], twiddle[1, l : l + 1, cos_at]
            spread[here, cos_at] = (tw_c * sum_c + tw_s * sum_s).astype(jnp.bfloat16)
            spread[here, sin_at] = (tw_c * sum_s - tw_s * sum_c).astype(jnp.bfloat16)

    transform(0)
    for t in range(K // KT):
        if t + 1 < K // KT:
            transform(t + 1)
        twist(t)
    for here in (slice(0, half), slice(half, total)):
        result[here] = jnp.dot(spread[here], table_t[...], preferred_element_type=jnp.float32)


def shift_rows(cells, down, edge):
    row = lax.broadcasted_iota(jnp.int32, cells.shape, 0)
    last = cells.shape[0] - 1
    if down:
        return jnp.where(row == 0, edge, pltpu.roll(cells, 1, 0))
    return jnp.where(row == last, edge, pltpu.roll(cells, last, 0))


def shift_cols(cells, right, edge):
    lane = lax.broadcasted_iota(jnp.int32, cells.shape, 1)
    last = cells.shape[1] - 1
    if right:
        return jnp.where(lane == 0, edge, pltpu.roll(cells, 1, 1))
    return jnp.where(lane == last, edge, pltpu.roll(cells, last, 1))


def window_kernel(
    n_ref, nu_hbm, src_hbm, dst_hbm, live_hbm, force_hbm, mix_hbm, mask_hbm, weight_hbm, u_hbm, v_hbm,
    out_ocean, out_u, out_v,
    nu_ref, src_ref, dst_ref, live_ref, force, mix, mask, weight, last_u, load_sem,
    cells, ratio, ocean, send_n, send_s, send_w, send_e, got_n, got_s, got_w, got_e, halo_send, halo_recv,
    flux, note, notes, note_send, note_recv,
    stage, got_u, got_v, fwd_send, fwd_recv,
    coarse, fine, coarse_t, fine_t, table, table_t, twiddle,
    packed, raw, spread, result, back_u, back_v, blank, back_send, back_recv, ocean_sem,
):
    me, oc = lax.axis_index("lon"), lax.axis_index("ocn")
    n_lon, n_ocn = lax.axis_size("lon"), lax.axis_size("ocn")
    levels = cells.shape[0] - 1
    last_owner = n_lon - 1
    share = 2
    source = me < NBLK

    def mine(t):
        return pl.ds(share * t, share)

    loads = [
        pltpu.make_async_copy(force_hbm, force, load_sem.at[0]),
        pltpu.make_async_copy(mix_hbm, mix, load_sem.at[1]),
        pltpu.make_async_copy(mask_hbm, mask, load_sem.at[2]),
        pltpu.make_async_copy(weight_hbm.at[pl.ds(0, NBLK)], weight, load_sem.at[3]),
        pltpu.make_async_copy(u_hbm.at[mine(last_owner)], last_u, load_sem.at[4]),
        pltpu.make_async_copy(nu_hbm, nu_ref, load_sem.at[5]),
        pltpu.make_async_copy(src_hbm, src_ref, load_sem.at[6]),
        pltpu.make_async_copy(dst_hbm, dst_ref, load_sem.at[7]),
        pltpu.make_async_copy(live_hbm, live_ref, load_sem.at[8]),
    ]
    for load in loads:
        load.start()

    barrier = pltpu.get_barrier_semaphore()

    def greet(i, carry):
        pl.semaphore_signal(barrier, inc=1, device_id={"lon": lax.rem(me + i, n_lon)}, device_id_type=MESH)
        return carry

    lax.fori_loop(1, n_lon, greet, 0)

    @pl.when(oc > 0)
    def _():
        pl.semaphore_signal(barrier, inc=1, device_id={"ocn": oc - 1}, device_id_type=MESH)

    @pl.when(oc < n_ocn - 1)
    def _():
        pl.semaphore_signal(barrier, inc=1, device_id={"ocn": oc + 1}, device_id_type=MESH)

    points = n_ref[0].astype(jnp.float32)
    build_tables(points, coarse, fine, coarse_t, fine_t, table, table_t, twiddle)

    for load in loads[:3]:
        load.wait()
    zero = jnp.zeros(force.shape[1:], jnp.float32)
    rat, val, below = zero, zero, zero
    for z in range(levels - 1, -1, -1):
        above = mix[z - 1] if z > 0 else zero
        inv = 1.0 / (1.0 + above + below * (1.0 - rat))
        val = (force[z] + below * val) * inv
        rat = above * inv
        cells[z] = val
        ratio[z] = rat
        below = above
    lane = lax.broadcasted_iota(jnp.int32, zero.shape, 1)
    west, east = zero, zero
    send_n[pl.ds(levels, 8), :] = zero
    send_s[pl.ds(levels, 8), :] = zero
    s = zero
    for z in range(levels + 1):
        if z < levels:
            s = cells[z] + ratio[z] * s if z > 0 else cells[0]
        else:
            s = mask[...].astype(jnp.float32)
        cells[z] = s
        send_n[z : z + 1, :] = s[0:1, :]
        send_s[z : z + 1, :] = s[7:8, :]
        west = jnp.where(lane == z, jnp.broadcast_to(s[:, 0:1], s.shape), west)
        east = jnp.where(lane == z, jnp.broadcast_to(s[:, BLK - 1 : BLK], s.shape), east)
    send_w[...] = west
    send_e[...] = east

    pl.semaphore_wait(barrier, n_lon - 1 + (oc > 0).astype(jnp.int32) + (oc < n_ocn - 1).astype(jnp.int32))

    sides = (
        (oc > 0, oc < n_ocn - 1, {"ocn": oc - 1}, send_n, got_s),
        (oc < n_ocn - 1, oc > 0, {"ocn": oc + 1}, send_s, got_n),
        (me > 0, me < n_lon - 1, {"lon": me - 1}, send_w, got_e),
        (me < n_lon - 1, me > 0, {"lon": me + 1}, send_e, got_w),
    )

    def halo(i):
        has, gets, where, out, into = sides[i]
        return has, gets, into, pltpu.make_async_remote_copy(
            src_ref=out, dst_ref=into, send_sem=halo_send.at[i], recv_sem=halo_recv.at[i], device_id=where, device_id_type=MESH
        )

    for i in range(4):
        has, gets, into, copy = halo(i)
        pl.when(has)(copy.start)

        @pl.when(jnp.logical_not(gets))
        def _(into=into):
            into[...] = jnp.zeros_like(into)

    def forward(i, carry):
        t = lax.rem(me + i, n_lon)
        pltpu.make_async_remote_copy(
            src_ref=v_hbm.at[mine(t)], dst_ref=got_v.at[me], send_sem=fwd_send.at[0], recv_sem=fwd_recv.at[0], device_id={"lon": t}, device_id_type=MESH
        ).start()

        @pl.when(t != last_owner)
        def _():
            pltpu.make_async_remote_copy(
                src_ref=u_hbm.at[mine(t)], dst_ref=got_u.at[me], send_sem=fwd_send.at[1], recv_sem=fwd_recv.at[1], device_id={"lon": t}, device_id_type=MESH
            ).start()

        return carry

    @pl.when(source)
    def _():
        lax.fori_loop(1, n_lon, forward, 0)
        pltpu.make_async_copy(v_hbm.at[mine(me)], got_v.at[me], fwd_recv.at[0]).start()
        pltpu.make_async_copy(u_hbm.at[mine(me)], got_u.at[me], fwd_recv.at[1]).start()

    for i in range(4):
        has, gets, into, copy = halo(i)
        pl.when(gets)(copy.wait_recv)
        pl.when(has)(copy.wait_send)

    m = cells[levels]
    m_n, m_s = shift_rows(m, True, got_n[levels : levels + 1, :]), shift_rows(m, False, got_s[levels : levels + 1, :])
    m_w = shift_cols(m, True, jnp.broadcast_to(got_w[:, levels : levels + 1], m.shape))
    m_e = shift_cols(m, False, jnp.broadcast_to(got_e[:, levels : levels + 1], m.shape))

    def mixed(z):
        s = cells[z]
        near = m_n * (shift_rows(s, True, got_n[z : z + 1, :]) - s)
        near += m_s * (shift_rows(s, False, got_s[z : z + 1, :]) - s)
        near += m_w * (shift_cols(s, True, jnp.broadcast_to(got_w[:, z : z + 1], s.shape)) - s)
        near += m_e * (shift_cols(s, False, jnp.broadcast_to(got_e[:, z : z + 1], s.shape)) - s)
        return m * (s + NU_MIX * near)

    surface = mixed(0)
    ocean[0] = surface
    flux[...] = surface.astype(jnp.bfloat16).astype(jnp.float32)
    for load in loads[3:4] + loads[6:]:
        load.wait()

    def owner(p, carry):
        one = flux[pl.ds(src_ref[0, p], 1), :]
        two = flux[pl.ds(src_ref[1, p], 1), :]
        row = lax.broadcasted_iota(jnp.int32, (8, BLK), 0)
        lhs = jnp.concatenate([jnp.where(row == 0, one, 0.0), jnp.where(row == 1, two, 0.0)], 1).astype(jnp.bfloat16)
        both = jnp.concatenate([weight[p, 0], weight[p, 1]], 1)
        got = lax.dot_general(lhs, both, (((1,), (1,)), ((), ())), preferred_element_type=jnp.float32)
        code_0 = live_ref[0, p] * (dst_ref[0, p] + 1) - 1
        code_1 = live_ref[1, p] * (dst_ref[1, p] + 1) - 1
        codes = jnp.where(row == 2, code_0, code_1).astype(jnp.float32)
        note[p] = jnp.where(row < 2, got, codes)[0:4]
        return carry

    lax.fori_loop(0, NBLK, owner, 0, unroll=3)

    def tell(p, carry):
        @pl.when(p != me)
        def _():
            pltpu.make_async_remote_copy(
                src_ref=note.at[p], dst_ref=notes.at[me], send_sem=note_send, recv_sem=note_recv, device_id={"lon": p}, device_id_type=MESH
            ).start()

        return carry

    lax.fori_loop(0, NBLK, tell, 0)

    @pl.when(source)
    def _():
        pltpu.make_async_copy(note.at[me], notes.at[me], note_recv).start()

    for z in range(1, levels):
        ocean[z] = mixed(z)
    ocean_copy = pltpu.make_async_copy(ocean, out_ocean, ocean_sem)
    ocean_copy.start()
    loads[4].wait()

    @pl.when(source)
    def _():
        pltpu.make_async_copy(notes, notes, note_recv).wait()
        even = 2.0 * iota((8, BLK), 0)
        odd = even + 1.0

        def add(l, sums):
            sum_even, sum_odd = sums
            block = notes[l]
            for c in range(2):
                value, code = block[c : c + 1, :], block[c + 2 : c + 3, :]
                sum_even += jnp.where(code == even, value, 0.0)
                sum_odd += jnp.where(code == odd, value, 0.0)
            return sum_even, sum_odd

        blank_sum = jnp.zeros((8, BLK), jnp.float32)
        sum_even, sum_odd = lax.fori_loop(0, n_lon, add, (blank_sum, blank_sum), unroll=4)
        coupling = jnp.concatenate([sum_even, sum_odd], 1)
        stage[0] = last_u[0]
        stage[1] = (last_u[1].astype(jnp.float32) + coupling).astype(jnp.bfloat16)
        pltpu.make_async_remote_copy(
            src_ref=stage, dst_ref=got_u.at[me], send_sem=fwd_send.at[1], recv_sem=fwd_recv.at[1], device_id={"lon": last_owner}, device_id_type=MESH
        ).start()

    loads[5].wait()
    column = iota((16, SEGLON), 1)
    row = iota((16, KT), 0)
    nu = jnp.where(row < 8, nu_ref[share * me], nu_ref[share * me + 1])
    for f, (got, back, out) in enumerate(((got_v, back_v, out_v), (got_u, back_u, out_u))):
        pltpu.make_async_copy(got, got, fwd_recv.at[f]).wait()

        def pack(l, carry, got=got):
            inside = column + (l * SEGLON).astype(jnp.float32) < points
            block = got[l].astype(jnp.float32).reshape(16, SEGLON)
            packed[pl.ds(pl.multiple_of(16 * l, 16), 16), :] = jnp.where(inside, block, 0.0).astype(jnp.bfloat16)
            return carry

        lax.fori_loop(0, NBLK, pack, 0)
        spectral(16, points, nu, packed, table, table_t, twiddle, raw, spread, result)

        def unpack(l, carry, back=back, out=out, f=f):
            inside = column + (l * SEGLON).astype(jnp.float32) < points
            block = result[pl.ds(pl.multiple_of(16 * l, 16), 16), :]
            back[l] = jnp.where(inside, block, 0.0).reshape(2, 8, SEGLON).astype(jnp.bfloat16)

            @pl.when(l != me)
            def _():
                pltpu.make_async_remote_copy(
                    src_ref=back.at[l], dst_ref=out.at[mine(me)], send_sem=back_send.at[f], recv_sem=back_recv.at[f], device_id={"lon": l}, device_id_type=MESH
                ).start()

            return carry

        lax.fori_loop(0, NBLK, unpack, 0)

        @pl.when(source)
        def _(back=back, out=out, f=f):
            pltpu.make_async_copy(back.at[me], out.at[mine(me)], back_recv.at[f]).start()

        @pl.when(jnp.logical_not(source))
        def _(back=back, out=out, f=f):
            if f == 0:
                blank[...] = jnp.zeros_like(blank)
            pltpu.make_async_copy(blank, out, back_recv.at[f]).start()

    ocean_copy.wait()

    @pl.when(source)
    def _():
        for f in range(2):
            sent = v_hbm.at[pl.ds(0, share * (n_lon - 1))]
            pltpu.make_async_copy(sent, sent, fwd_send.at[f]).wait()
        told = note.at[pl.ds(0, NBLK - 1)]
        pltpu.make_async_copy(told, told, note_send).wait()

    @pl.when(jnp.logical_not(source))
    def _():
        pltpu.make_async_copy(note, note, note_send).wait()

    for f, (back, out) in enumerate(((back_v, out_v), (back_u, out_u))):

        @pl.when(source)
        def _(back=back, f=f):
            sent = back.at[pl.ds(0, NBLK - 1)]
            pltpu.make_async_copy(sent, sent, back_send.at[f]).wait()

        @pl.when(jnp.logical_not(source))
        def _(back=back, f=f):
            pltpu.make_async_copy(back, back, back_send.at[f]).wait()

        pltpu.make_async_copy(out, out, back_recv.at[f]).wait()


def finish_kernel(ocean_in, u_in, v_in, ocean_out, u_out, v_out, sems):
    pairs = ((ocean_in, ocean_out), (u_in, u_out), (v_in, v_out))
    copies = [pltpu.make_async_copy(here, there, sems.at[i]) for i, (here, there) in enumerate(pairs)]
    for copy in copies:
        copy.start()
    for copy in copies:
        copy.wait()


def per_device(
    ocean_adjoint,
    mixing_coef,
    land_mask,
    remap_src,
    remap_dst,
    remap_live,
    remap_weight,
    atm_u,
    atm_v,
    spectral_nu,
    band_points,
):
    lon_devices = lax.axis_size("lon")
    levels = ocean_adjoint.shape[0]
    slots = remap_src.shape[2:]
    tile = ocean_adjoint.shape[1:]
    m = 16 * NBLK
    f32, bf16, dma = jnp.float32, jnp.bfloat16, pltpu.SemaphoreType.DMA
    smem = pl.BlockSpec(memory_space=pltpu.SMEM)
    hbm = pl.BlockSpec(memory_space=pltpu.HBM)
    anywhere = pl.BlockSpec(memory_space=pl.ANY)
    two = (2,) + atm_u.shape[1:]
    edge = (levels + 8, BLK)
    shapes = (
        jax.ShapeDtypeStruct(ocean_adjoint.shape, f32),
        jax.ShapeDtypeStruct(atm_u.shape, bf16),
        jax.ShapeDtypeStruct(atm_v.shape, bf16),
    )
    results = pl.pallas_call(
        window_kernel,
        out_shape=shapes,
        in_specs=[smem] + [hbm] * 10,
        out_specs=(anywhere, anywhere, anywhere),
        scratch_shapes=[
            pltpu.SMEM(spectral_nu.shape, f32),
            pltpu.SMEM(slots[::-1], jnp.int32),
            pltpu.SMEM(slots[::-1], jnp.int32),
            pltpu.SMEM(slots[::-1], jnp.int32),
            pltpu.VMEM(ocean_adjoint.shape, f32),
            pltpu.VMEM(mixing_coef.shape, f32),
            pltpu.VMEM(land_mask.shape, jnp.int32),
            pltpu.VMEM((NBLK, slots[1], BLK, BLK), bf16),
            pltpu.VMEM(two, bf16),
            dma((9,)),
            pltpu.VMEM((levels + 1,) + tile, f32),
            pltpu.VMEM((levels,) + tile, f32),
            pltpu.VMEM((levels,) + tile, f32),
            pltpu.VMEM(edge, f32),
            pltpu.VMEM(edge, f32),
            pltpu.VMEM(tile, f32),
            pltpu.VMEM(tile, f32),
            pltpu.VMEM(edge, f32),
            pltpu.VMEM(edge, f32),
            pltpu.VMEM(tile, f32),
            pltpu.VMEM(tile, f32),
            dma((4,)),
            dma((4,)),
            pltpu.VMEM(tile, f32),
            pltpu.VMEM((NBLK, 4, BLK), f32),
            pltpu.VMEM((lon_devices, 4, BLK), f32),
            dma,
            dma,
            pltpu.VMEM(two, bf16),
            pltpu.VMEM((NBLK,) + two, bf16),
            pltpu.VMEM((NBLK,) + two, bf16),
            dma((2,)),
            dma((2,)),
            pltpu.VMEM((2, 16, K), f32),
            pltpu.VMEM((2, 16, K), f32),
            pltpu.VMEM((2, K // 16, SEGLON), f32),
            pltpu.VMEM((2, 16, SEGLON), f32),
            pltpu.VMEM((SEGLON, 2 * K), bf16),
            pltpu.VMEM((2 * K, SEGLON), bf16),
            pltpu.VMEM((2, TWROWS, K), f32),
            pltpu.VMEM((m, SEGLON), bf16),
            pltpu.VMEM((K // KT, 2, m, KT), f32),
            pltpu.VMEM((m, 2 * K), bf16),
            pltpu.VMEM((m, SEGLON), f32),
            pltpu.VMEM((NBLK,) + two, bf16),
            pltpu.VMEM((NBLK,) + two, bf16),
            pltpu.VMEM(atm_u.shape, bf16),
            dma((2,)),
            dma((2,)),
            dma,
        ],
        compiler_params=pltpu.CompilerParams(collective_id=0, has_side_effects=True),
        name="window",
    )(
        band_points,
        spectral_nu,
        remap_src.reshape(slots).T,
        remap_dst.reshape(slots).T,
        remap_live.reshape(slots).T,
        ocean_adjoint,
        mixing_coef,
        land_mask,
        remap_weight.reshape(remap_weight.shape[2:]),
        atm_u,
        atm_v,
    )
    return pl.pallas_call(
        finish_kernel,
        out_shape=shapes,
        in_specs=[anywhere] * 3,
        out_specs=(hbm, hbm, hbm),
        scratch_shapes=[dma((3,))],
        name="finish",
    )(*results)


def solution(mesh):
    placed = (
        P(None, "ocn", "lon"),
        P(None, "ocn", "lon"),
        P("ocn", "lon"),
        P("ocn", "lon", None, None),
        P("ocn", "lon", None, None),
        P("ocn", "lon", None, None),
        P("ocn", "lon", None, None, None, None),
        P(None, "ocn", "lon"),
        P(None, "ocn", "lon"),
        P(),
        P("ocn"),
    )
    return jax.shard_map(
        per_device,
        mesh=mesh,
        in_specs=placed,
        out_specs=(P(None, "ocn", "lon"), P(None, "ocn", "lon"), P(None, "ocn", "lon")),
        check_vma=False,
    )
```

```python
import math

import jax
import jax.numpy as jnp
from jax import lax
from jax.experimental import pallas as pl
from jax.experimental.pallas import tpu as pltpu
from jax.sharding import PartitionSpec as P

K = 1280
BLK = 128
SEGLON = 256
NBLK = 21
TWROWS = 24
KT = 256
NU_MIX = 0.2
MESH = pl.DeviceIdType.MESH

COS_C = [(-1.0) ** m * (2.0 * math.pi) ** (2 * m) / math.factorial(2 * m) for m in range(11)]
SIN_C = [(-1.0) ** m * (2.0 * math.pi) ** (2 * m + 1) / math.factorial(2 * m + 1) for m in range(11)]


def iota(shape, dim):
    return lax.broadcasted_iota(jnp.int32, shape, dim).astype(jnp.float32)


def cos_sin(steps, points):
    inverse = 1.0 / points
    turns = jnp.floor(steps * inverse + 0.5)
    part = (steps - turns * points) * inverse
    square = part * part
    cosine = jnp.full_like(square, COS_C[10])
    sine = jnp.full_like(square, SIN_C[10])
    for m in range(9, -1, -1):
        cosine = cosine * square + COS_C[m]
        sine = sine * square + SIN_C[m]
    return cosine, sine * part


def build_tables(points, coarse, fine, coarse_t, fine_t, table, table_t, twiddle):
    n_row = jnp.full((16, K), points, jnp.float32)
    step_row, wave_row = iota((16, K), 0), iota((16, K), 1)
    coarse[0], coarse[1] = cos_sin(16.0 * step_row * wave_row, n_row)
    fine[0], fine[1] = cos_sin(step_row * wave_row, n_row)
    n_tw = jnp.full((TWROWS, K), points, jnp.float32)
    twiddle[0], twiddle[1] = cos_sin(float(SEGLON) * iota((TWROWS, K), 0) * iota((TWROWS, K), 1), n_tw)
    n_t = jnp.full((K // 16, SEGLON), points, jnp.float32)
    coarse_t[0], coarse_t[1] = cos_sin(16.0 * iota((K // 16, SEGLON), 0) * iota((K // 16, SEGLON), 1), n_t)
    n_f = jnp.full((16, SEGLON), points, jnp.float32)
    fine_t[0], fine_t[1] = cos_sin(iota((16, SEGLON), 0) * iota((16, SEGLON), 1), n_f)

    def rows(p, carry):
        cos_p, sin_p = coarse[0, pl.ds(p, 1), :], coarse[1, pl.ds(p, 1), :]
        here = pl.ds(pl.multiple_of(16 * p, 16), 16)
        table[here, 0:K] = (cos_p * fine[0] - sin_p * fine[1]).astype(jnp.bfloat16)
        table[here, K : 2 * K] = (sin_p * fine[0] + cos_p * fine[1]).astype(jnp.bfloat16)
        return carry

    lax.fori_loop(0, SEGLON // 16, rows, 0)

    def rows_t(p, carry):
        cos_p, sin_p = coarse_t[0, pl.ds(p, 1), :], coarse_t[1, pl.ds(p, 1), :]
        here = pl.ds(pl.multiple_of(16 * p, 16), 16)
        table_t[here, :] = (cos_p * fine_t[0] - sin_p * fine_t[1]).astype(jnp.bfloat16)
        table_t[pl.ds(pl.multiple_of(K + 16 * p, 16), 16), :] = (sin_p * fine_t[0] + cos_p * fine_t[1]).astype(jnp.bfloat16)
        return carry

    lax.fori_loop(0, K // 16, rows_t, 0, unroll=2)


def spectral(rows, points, viscosity, packed, table, table_t, twiddle, raw, spread, result):
    total = NBLK * rows
    half = (total // 2 + 15) // 16 * 16
    scale = 2.0 / jnp.full((rows, KT), points, jnp.float32)

    def transform(t):
        for part in range(2):
            at = part * K + t * KT
            raw[t, part] = jnp.dot(packed[...], table[:, at : at + KT], preferred_element_type=jnp.float32)

    def twist(t):
        cos_at, sin_at = slice(t * KT, (t + 1) * KT), slice(K + t * KT, K + (t + 1) * KT)
        sum_c = jnp.zeros((rows, KT), jnp.float32)
        sum_s = jnp.zeros((rows, KT), jnp.float32)
        for l in range(NBLK):
            here = slice(l * rows, (l + 1) * rows)
            part_c, part_s = raw[t, 0, here, :], raw[t, 1, here, :]
            tw_c, tw_s = twiddle[0, l : l + 1, cos_at], twiddle[1, l : l + 1, cos_at]
            sum_c += tw_c * part_c - tw_s * part_s
            sum_s += tw_s * part_c + tw_c * part_s
        ratio = (iota((rows, KT), 1) + float(t * KT)) * (1.0 / K)
        damping = scale / (1.0 + viscosity * ratio * ratio)
        sum_c *= damping
        sum_s *= damping
        for l in range(NBLK):
            here = slice(l * rows, (l + 1) * rows)
            tw_c, tw_s = twiddle[0, l : l + 1, cos_at], twiddle[1, l : l + 1, cos_at]
            spread[here, cos_at] = (tw_c * sum_c + tw_s * sum_s).astype(jnp.bfloat16)
            spread[here, sin_at] = (tw_c * sum_s - tw_s * sum_c).astype(jnp.bfloat16)

    transform(0)
    for t in range(K // KT):
        if t + 1 < K // KT:
            transform(t + 1)
        twist(t)
    for here in (slice(0, half), slice(half, total)):
        result[here] = jnp.dot(spread[here], table_t[...], preferred_element_type=jnp.float32)


def shift_rows(cells, down, edge):
    row = lax.broadcasted_iota(jnp.int32, cells.shape, 0)
    last = cells.shape[0] - 1
    if down:
        return jnp.where(row == 0, edge, pltpu.roll(cells, 1, 0))
    return jnp.where(row == last, edge, pltpu.roll(cells, last, 0))


def shift_cols(cells, right, edge):
    lane = lax.broadcasted_iota(jnp.int32, cells.shape, 1)
    last = cells.shape[1] - 1
    if right:
        return jnp.where(lane == 0, edge, pltpu.roll(cells, 1, 1))
    return jnp.where(lane == last, edge, pltpu.roll(cells, last, 1))


def window_kernel(
    n_ref, nu_hbm, src_hbm, dst_hbm, live_hbm, force_hbm, mix_hbm, mask_hbm, weight_hbm, u_hbm, v_hbm,
    out_ocean, out_u, out_v,
    nu_ref, src_ref, dst_ref, live_ref, force, mix, mask, weight, last_u, load_sem,
    cells, ratio, ocean, send_n, send_s, send_w, send_e, got_n, got_s, got_w, got_e, halo_send, halo_recv,
    flux, note, notes, note_send, note_recv,
    stage, got_u, got_v, fwd_send, fwd_recv,
    coarse, fine, coarse_t, fine_t, table, table_t, twiddle,
    packed, raw, spread, result, back_u, back_v, blank, back_send, back_recv, ocean_sem,
):
    me, oc = lax.axis_index("lon"), lax.axis_index("ocn")
    n_lon, n_ocn = lax.axis_size("lon"), lax.axis_size("ocn")
    levels = cells.shape[0] - 1
    last_owner = n_lon - 1
    share = 2
    source = me < NBLK

    def mine(t):
        return pl.ds(share * t, share)

    loads = [
        pltpu.make_async_copy(force_hbm, force, load_sem.at[0]),
        pltpu.make_async_copy(mix_hbm, mix, load_sem.at[1]),
        pltpu.make_async_copy(mask_hbm, mask, load_sem.at[2]),
        pltpu.make_async_copy(weight_hbm.at[pl.ds(0, NBLK)], weight, load_sem.at[3]),
        pltpu.make_async_copy(u_hbm.at[mine(last_owner)], last_u, load_sem.at[4]),
        pltpu.make_async_copy(nu_hbm, nu_ref, load_sem.at[5]),
        pltpu.make_async_copy(src_hbm, src_ref, load_sem.at[6]),
        pltpu.make_async_copy(dst_hbm, dst_ref, load_sem.at[7]),
        pltpu.make_async_copy(live_hbm, live_ref, load_sem.at[8]),
    ]
    for load in loads:
        load.start()

    barrier = pltpu.get_barrier_semaphore()

    def greet(i, carry):
        pl.semaphore_signal(barrier, inc=1, device_id={"lon": lax.rem(me + i, n_lon)}, device_id_type=MESH)
        return carry

    lax.fori_loop(1, n_lon, greet, 0)

    @pl.when(oc > 0)
    def _():
        pl.semaphore_signal(barrier, inc=1, device_id={"ocn": oc - 1}, device_id_type=MESH)

    @pl.when(oc < n_ocn - 1)
    def _():
        pl.semaphore_signal(barrier, inc=1, device_id={"ocn": oc + 1}, device_id_type=MESH)

    for load in loads[:3]:
        load.wait()
    zero = jnp.zeros(force.shape[1:], jnp.float32)
    rat, val, below = zero, zero, zero
    for z in range(levels - 1, -1, -1):
        above = mix[z - 1] if z > 0 else zero
        inv = 1.0 / (1.0 + above + below * (1.0 - rat))
        val = (force[z] + below * val) * inv
        rat = above * inv
        cells[z] = val
        ratio[z] = rat
        below = above
    lane = lax.broadcasted_iota(jnp.int32, zero.shape, 1)
    west, east = zero, zero
    send_n[pl.ds(levels, 8), :] = zero
    send_s[pl.ds(levels, 8), :] = zero
    s = zero
    for z in range(levels + 1):
        if z < levels:
            s = cells[z] + ratio[z] * s if z > 0 else cells[0]
        else:
            s = mask[...].astype(jnp.float32)
        cells[z] = s
        send_n[z : z + 1, :] = s[0:1, :]
        send_s[z : z + 1, :] = s[7:8, :]
        west = jnp.where(lane == z, jnp.broadcast_to(s[:, 0:1], s.shape), west)
        east = jnp.where(lane == z, jnp.broadcast_to(s[:, BLK - 1 : BLK], s.shape), east)
    send_w[...] = west
    send_e[...] = east

    pl.semaphore_wait(barrier, n_lon - 1 + (oc > 0).astype(jnp.int32) + (oc < n_ocn - 1).astype(jnp.int32))

    sides = (
        (oc > 0, oc < n_ocn - 1, {"ocn": oc - 1}, send_n, got_s),
        (oc < n_ocn - 1, oc > 0, {"ocn": oc + 1}, send_s, got_n),
        (me > 0, me < n_lon - 1, {"lon": me - 1}, send_w, got_e),
        (me < n_lon - 1, me > 0, {"lon": me + 1}, send_e, got_w),
    )

    def halo(i):
        has, gets, where, out, into = sides[i]
        return has, gets, into, pltpu.make_async_remote_copy(
            src_ref=out, dst_ref=into, send_sem=halo_send.at[i], recv_sem=halo_recv.at[i], device_id=where, device_id_type=MESH
        )

    for i in range(4):
        has, gets, into, copy = halo(i)
        pl.when(has)(copy.start)

        @pl.when(jnp.logical_not(gets))
        def _(into=into):
            into[...] = jnp.zeros_like(into)

    def send_rows(f, field, got):
        def forward(i, carry):
            t = lax.rem(me + i, n_lon)

            def start():
                pltpu.make_async_remote_copy(
                    src_ref=field.at[mine(t)], dst_ref=got.at[me], send_sem=fwd_send.at[f], recv_sem=fwd_recv.at[f], device_id={"lon": t}, device_id_type=MESH
                ).start()

            if f == 0:
                start()
            else:
                pl.when(t != last_owner)(start)
            return carry

        @pl.when(source)
        def _():
            lax.fori_loop(1, n_lon, forward, 0)
            pltpu.make_async_copy(field.at[mine(me)], got.at[me], fwd_recv.at[f]).start()

    send_rows(0, v_hbm, got_v)

    points = n_ref[0].astype(jnp.float32)
    build_tables(points, coarse, fine, coarse_t, fine_t, table, table_t, twiddle)

    for i in range(4):
        has, gets, into, copy = halo(i)
        pl.when(gets)(copy.wait_recv)
        pl.when(has)(copy.wait_send)

    m = cells[levels]
    m_n, m_s = shift_rows(m, True, got_n[levels : levels + 1, :]), shift_rows(m, False, got_s[levels : levels + 1, :])
    m_w = shift_cols(m, True, jnp.broadcast_to(got_w[:, levels : levels + 1], m.shape))
    m_e = shift_cols(m, False, jnp.broadcast_to(got_e[:, levels : levels + 1], m.shape))

    def mixed(z):
        s = cells[z]
        near = m_n * (shift_rows(s, True, got_n[z : z + 1, :]) - s)
        near += m_s * (shift_rows(s, False, got_s[z : z + 1, :]) - s)
        near += m_w * (shift_cols(s, True, jnp.broadcast_to(got_w[:, z : z + 1], s.shape)) - s)
        near += m_e * (shift_cols(s, False, jnp.broadcast_to(got_e[:, z : z + 1], s.shape)) - s)
        return m * (s + NU_MIX * near)

    surface = mixed(0)
    ocean[0] = surface
    flux[...] = surface.astype(jnp.bfloat16).astype(jnp.float32)
    for load in loads[3:4] + loads[6:]:
        load.wait()

    def owner(p, carry):
        one = flux[pl.ds(src_ref[0, p], 1), :]
        two = flux[pl.ds(src_ref[1, p], 1), :]
        row = lax.broadcasted_iota(jnp.int32, (8, BLK), 0)
        lhs = jnp.concatenate([jnp.where(row == 0, one, 0.0), jnp.where(row == 1, two, 0.0)], 1).astype(jnp.bfloat16)
        both = jnp.concatenate([weight[p, 0], weight[p, 1]], 1)
        got = lax.dot_general(lhs, both, (((1,), (1,)), ((), ())), preferred_element_type=jnp.float32)
        code_0 = live_ref[0, p] * (dst_ref[0, p] + 1) - 1
        code_1 = live_ref[1, p] * (dst_ref[1, p] + 1) - 1
        codes = jnp.where(row == 2, code_0, code_1).astype(jnp.float32)
        note[p] = jnp.where(row < 2, got, codes)[0:4]
        return carry

    lax.fori_loop(0, NBLK, owner, 0, unroll=3)

    def tell(p, carry):
        @pl.when(p != me)
        def _():
            pltpu.make_async_remote_copy(
                src_ref=note.at[p], dst_ref=notes.at[me], send_sem=note_send, recv_sem=note_recv, device_id={"lon": p}, device_id_type=MESH
            ).start()

        return carry

    lax.fori_loop(0, NBLK, tell, 0)

    @pl.when(source)
    def _():
        pltpu.make_async_copy(note.at[me], notes.at[me], note_recv).start()

    send_rows(1, u_hbm, got_u)
    for z in range(1, levels):
        ocean[z] = mixed(z)
    ocean_copy = pltpu.make_async_copy(ocean, out_ocean, ocean_sem)
    ocean_copy.start()
    loads[4].wait()

    @pl.when(source)
    def _():
        pltpu.make_async_copy(notes, notes, note_recv).wait()
        even = 2.0 * iota((8, BLK), 0)
        odd = even + 1.0

        def add(l, sums):
            sum_even, sum_odd = sums
            block = notes[l]
            for c in range(2):
                value, code = block[c : c + 1, :], block[c + 2 : c + 3, :]
                sum_even += jnp.where(code == even, value, 0.0)
                sum_odd += jnp.where(code == odd, value, 0.0)
            return sum_even, sum_odd

        blank_sum = jnp.zeros((8, BLK), jnp.float32)
        sum_even, sum_odd = lax.fori_loop(0, n_lon, add, (blank_sum, blank_sum), unroll=4)
        coupling = jnp.concatenate([sum_even, sum_odd], 1)
        stage[0] = last_u[0]
        stage[1] = (last_u[1].astype(jnp.float32) + coupling).astype(jnp.bfloat16)
        pltpu.make_async_remote_copy(
            src_ref=stage, dst_ref=got_u.at[me], send_sem=fwd_send.at[1], recv_sem=fwd_recv.at[1], device_id={"lon": last_owner}, device_id_type=MESH
        ).start()

    loads[5].wait()
    column = iota((16, SEGLON), 1)
    row = iota((16, KT), 0)
    nu = jnp.where(row < 8, nu_ref[share * me], nu_ref[share * me + 1])
    for f, (got, back, out) in enumerate(((got_v, back_v, out_v), (got_u, back_u, out_u))):
        pltpu.make_async_copy(got, got, fwd_recv.at[f]).wait()

        def pack(l, carry, got=got):
            inside = column + (l * SEGLON).astype(jnp.float32) < points
            block = got[l].astype(jnp.float32).reshape(16, SEGLON)
            packed[pl.ds(pl.multiple_of(16 * l, 16), 16), :] = jnp.where(inside, block, 0.0).astype(jnp.bfloat16)
            return carry

        lax.fori_loop(0, NBLK, pack, 0)
        spectral(16, points, nu, packed, table, table_t, twiddle, raw, spread, result)

        def unpack(l, carry, back=back, out=out, f=f):
            inside = column + (l * SEGLON).astype(jnp.float32) < points
            block = result[pl.ds(pl.multiple_of(16 * l, 16), 16), :]
            back[l] = jnp.where(inside, block, 0.0).reshape(2, 8, SEGLON).astype(jnp.bfloat16)

            @pl.when(l != me)
            def _():
                pltpu.make_async_remote_copy(
                    src_ref=back.at[l], dst_ref=out.at[mine(me)], send_sem=back_send.at[f], recv_sem=back_recv.at[f], device_id={"lon": l}, device_id_type=MESH
                ).start()

            return carry

        lax.fori_loop(0, NBLK, unpack, 0)

        @pl.when(source)
        def _(back=back, out=out, f=f):
            pltpu.make_async_copy(back.at[me], out.at[mine(me)], back_recv.at[f]).start()

        @pl.when(jnp.logical_not(source))
        def _(back=back, out=out, f=f):
            if f == 0:
                blank[...] = jnp.zeros_like(blank)
            pltpu.make_async_copy(blank, out, back_recv.at[f]).start()

    ocean_copy.wait()

    @pl.when(source)
    def _():
        for f in range(2):
            sent = v_hbm.at[pl.ds(0, share * (n_lon - 1))]
            pltpu.make_async_copy(sent, sent, fwd_send.at[f]).wait()
        told = note.at[pl.ds(0, NBLK - 1)]
        pltpu.make_async_copy(told, told, note_send).wait()

    @pl.when(jnp.logical_not(source))
    def _():
        pltpu.make_async_copy(note, note, note_send).wait()

    for f, (back, out) in enumerate(((back_v, out_v), (back_u, out_u))):

        @pl.when(source)
        def _(back=back, f=f):
            sent = back.at[pl.ds(0, NBLK - 1)]
            pltpu.make_async_copy(sent, sent, back_send.at[f]).wait()

        @pl.when(jnp.logical_not(source))
        def _(back=back, f=f):
            pltpu.make_async_copy(back, back, back_send.at[f]).wait()

        pltpu.make_async_copy(out, out, back_recv.at[f]).wait()


def finish_kernel(ocean_in, u_in, v_in, ocean_out, u_out, v_out, sems):
    pairs = ((ocean_in, ocean_out), (u_in, u_out), (v_in, v_out))
    copies = [pltpu.make_async_copy(here, there, sems.at[i]) for i, (here, there) in enumerate(pairs)]
    for copy in copies:
        copy.start()
    for copy in copies:
        copy.wait()


def per_device(
    ocean_adjoint,
    mixing_coef,
    land_mask,
    remap_src,
    remap_dst,
    remap_live,
    remap_weight,
    atm_u,
    atm_v,
    spectral_nu,
    band_points,
):
    lon_devices = lax.axis_size("lon")
    levels = ocean_adjoint.shape[0]
    slots = remap_src.shape[2:]
    tile = ocean_adjoint.shape[1:]
    m = 16 * NBLK
    f32, bf16, dma = jnp.float32, jnp.bfloat16, pltpu.SemaphoreType.DMA
    smem = pl.BlockSpec(memory_space=pltpu.SMEM)
    hbm = pl.BlockSpec(memory_space=pltpu.HBM)
    anywhere = pl.BlockSpec(memory_space=pl.ANY)
    two = (2,) + atm_u.shape[1:]
    edge = (levels + 8, BLK)
    shapes = (
        jax.ShapeDtypeStruct(ocean_adjoint.shape, f32),
        jax.ShapeDtypeStruct(atm_u.shape, bf16),
        jax.ShapeDtypeStruct(atm_v.shape, bf16),
    )
    results = pl.pallas_call(
        window_kernel,
        out_shape=tuple(pltpu.VMEM(x.shape, x.dtype) for x in shapes),
        in_specs=[smem] + [hbm] * 10,
        out_specs=(anywhere, anywhere, anywhere),
        scratch_shapes=[
            pltpu.SMEM(spectral_nu.shape, f32),
            pltpu.SMEM(slots[::-1], jnp.int32),
            pltpu.SMEM(slots[::-1], jnp.int32),
            pltpu.SMEM(slots[::-1], jnp.int32),
            pltpu.VMEM(ocean_adjoint.shape, f32),
            pltpu.VMEM(mixing_coef.shape, f32),
            pltpu.VMEM(land_mask.shape, jnp.int32),
            pltpu.VMEM((NBLK, slots[1], BLK, BLK), bf16),
            pltpu.VMEM(two, bf16),
            dma((9,)),
            pltpu.VMEM((levels + 1,) + tile, f32),
            pltpu.VMEM((levels,) + tile, f32),
            pltpu.VMEM((levels,) + tile, f32),
            pltpu.VMEM(edge, f32),
            pltpu.VMEM(edge, f32),
            pltpu.VMEM(tile, f32),
            pltpu.VMEM(tile, f32),
            pltpu.VMEM(edge, f32),
            pltpu.VMEM(edge, f32),
            pltpu.VMEM(tile, f32),
            pltpu.VMEM(tile, f32),
            dma((4,)),
            dma((4,)),
            pltpu.VMEM(tile, f32),
            pltpu.VMEM((NBLK, 4, BLK), f32),
            pltpu.VMEM((lon_devices, 4, BLK), f32),
            dma,
            dma,
            pltpu.VMEM(two, bf16),
            pltpu.VMEM((NBLK,) + two, bf16),
            pltpu.VMEM((NBLK,) + two, bf16),
            dma((2,)),
            dma((2,)),
            pltpu.VMEM((2, 16, K), f32),
            pltpu.VMEM((2, 16, K), f32),
            pltpu.VMEM((2, K // 16, SEGLON), f32),
            pltpu.VMEM((2, 16, SEGLON), f32),
            pltpu.VMEM((SEGLON, 2 * K), bf16),
            pltpu.VMEM((2 * K, SEGLON), bf16),
            pltpu.VMEM((2, TWROWS, K), f32),
            pltpu.VMEM((m, SEGLON), bf16),
            pltpu.VMEM((K // KT, 2, m, KT), f32),
            pltpu.VMEM((m, 2 * K), bf16),
            pltpu.VMEM((m, SEGLON), f32),
            pltpu.VMEM((NBLK,) + two, bf16),
            pltpu.VMEM((NBLK,) + two, bf16),
            pltpu.VMEM(atm_u.shape, bf16),
            dma((2,)),
            dma((2,)),
            dma,
        ],
        compiler_params=pltpu.CompilerParams(collective_id=0, has_side_effects=True),
        name="window",
    )(
        band_points,
        spectral_nu,
        remap_src.reshape(slots).T,
        remap_dst.reshape(slots).T,
        remap_live.reshape(slots).T,
        ocean_adjoint,
        mixing_coef,
        land_mask,
        remap_weight.reshape(remap_weight.shape[2:]),
        atm_u,
        atm_v,
    )
    return pl.pallas_call(
        finish_kernel,
        out_shape=shapes,
        in_specs=[pl.BlockSpec(memory_space=pltpu.VMEM)] * 3,
        out_specs=(hbm, hbm, hbm),
        scratch_shapes=[dma((3,))],
        compiler_params=pltpu.CompilerParams(vmem_limit_bytes=8 << 20),
        name="finish",
    )(*results)


def solution(mesh):
    placed = (
        P(None, "ocn", "lon"),
        P(None, "ocn", "lon"),
        P("ocn", "lon"),
        P("ocn", "lon", None, None),
        P("ocn", "lon", None, None),
        P("ocn", "lon", None, None),
        P("ocn", "lon", None, None, None, None),
        P(None, "ocn", "lon"),
        P(None, "ocn", "lon"),
        P(),
        P("ocn"),
    )
    return jax.shard_map(
        per_device,
        mesh=mesh,
        in_specs=placed,
        out_specs=(P(None, "ocn", "lon"), P(None, "ocn", "lon"), P(None, "ocn", "lon")),
        check_vma=False,
    )
```

```python
import math

import jax
import jax.numpy as jnp
from jax import lax
from jax.experimental import pallas as pl
from jax.experimental.pallas import tpu as pltpu
from jax.sharding import PartitionSpec as P

K = 1280
BLK = 128
SEGLON = 256
NBLK = 21
TWROWS = 24
KT = 256
NU_MIX = 0.2
MESH = pl.DeviceIdType.MESH

COS_C = [(-1.0) ** m * (2.0 * math.pi) ** (2 * m) / math.factorial(2 * m) for m in range(11)]
SIN_C = [(-1.0) ** m * (2.0 * math.pi) ** (2 * m + 1) / math.factorial(2 * m + 1) for m in range(11)]


def iota(shape, dim):
    return lax.broadcasted_iota(jnp.int32, shape, dim).astype(jnp.float32)


def cos_sin(steps, points):
    inverse = 1.0 / points
    turns = jnp.floor(steps * inverse + 0.5)
    part = (steps - turns * points) * inverse
    square = part * part
    cosine = jnp.full_like(square, COS_C[10])
    sine = jnp.full_like(square, SIN_C[10])
    for m in range(9, -1, -1):
        cosine = cosine * square + COS_C[m]
        sine = sine * square + SIN_C[m]
    return cosine, sine * part


def build_tables(points, coarse, fine, coarse_t, fine_t, table, table_t, twiddle):
    n_row = jnp.full((16, K), points, jnp.float32)
    step_row, wave_row = iota((16, K), 0), iota((16, K), 1)
    coarse[0], coarse[1] = cos_sin(16.0 * step_row * wave_row, n_row)
    fine[0], fine[1] = cos_sin(step_row * wave_row, n_row)
    n_tw = jnp.full((TWROWS, K), points, jnp.float32)
    twiddle[0], twiddle[1] = cos_sin(float(SEGLON) * iota((TWROWS, K), 0) * iota((TWROWS, K), 1), n_tw)
    n_t = jnp.full((K // 16, SEGLON), points, jnp.float32)
    coarse_t[0], coarse_t[1] = cos_sin(16.0 * iota((K // 16, SEGLON), 0) * iota((K // 16, SEGLON), 1), n_t)
    n_f = jnp.full((16, SEGLON), points, jnp.float32)
    fine_t[0], fine_t[1] = cos_sin(iota((16, SEGLON), 0) * iota((16, SEGLON), 1), n_f)

    def rows(p, carry):
        cos_p, sin_p = coarse[0, pl.ds(p, 1), :], coarse[1, pl.ds(p, 1), :]
        here = pl.ds(pl.multiple_of(16 * p, 16), 16)
        table[here, 0:K] = (cos_p * fine[0] - sin_p * fine[1]).astype(jnp.bfloat16)
        table[here, K : 2 * K] = (sin_p * fine[0] + cos_p * fine[1]).astype(jnp.bfloat16)
        return carry

    lax.fori_loop(0, SEGLON // 16, rows, 0)

    def rows_t(p, carry):
        cos_p, sin_p = coarse_t[0, pl.ds(p, 1), :], coarse_t[1, pl.ds(p, 1), :]
        here = pl.ds(pl.multiple_of(16 * p, 16), 16)
        table_t[here, :] = (cos_p * fine_t[0] - sin_p * fine_t[1]).astype(jnp.bfloat16)
        table_t[pl.ds(pl.multiple_of(K + 16 * p, 16), 16), :] = (sin_p * fine_t[0] + cos_p * fine_t[1]).astype(jnp.bfloat16)
        return carry

    lax.fori_loop(0, K // 16, rows_t, 0, unroll=2)


def spectral(rows, points, viscosity, packed, table, table_t, twiddle, raw, spread, result):
    total = NBLK * rows
    half = (total // 2 + 15) // 16 * 16
    scale = 2.0 / jnp.full((rows, KT), points, jnp.float32)

    def transform(t):
        for part in range(2):
            at = part * K + t * KT
            raw[t, part, 0:total, :] = jnp.dot(packed[0:total, :], table[:, at : at + KT], preferred_element_type=jnp.float32)

    def twist(t):
        cos_at, sin_at = slice(t * KT, (t + 1) * KT), slice(K + t * KT, K + (t + 1) * KT)
        sum_c = jnp.zeros((rows, KT), jnp.float32)
        sum_s = jnp.zeros((rows, KT), jnp.float32)
        for l in range(NBLK):
            here = slice(l * rows, (l + 1) * rows)
            part_c, part_s = raw[t, 0, here, :], raw[t, 1, here, :]
            tw_c, tw_s = twiddle[0, l : l + 1, cos_at], twiddle[1, l : l + 1, cos_at]
            sum_c += tw_c * part_c - tw_s * part_s
            sum_s += tw_s * part_c + tw_c * part_s
        ratio = (iota((rows, KT), 1) + float(t * KT)) * (1.0 / K)
        damping = scale / (1.0 + viscosity * ratio * ratio)
        sum_c *= damping
        sum_s *= damping
        for l in range(NBLK):
            here = slice(l * rows, (l + 1) * rows)
            tw_c, tw_s = twiddle[0, l : l + 1, cos_at], twiddle[1, l : l + 1, cos_at]
            spread[here, cos_at] = (tw_c * sum_c + tw_s * sum_s).astype(jnp.bfloat16)
            spread[here, sin_at] = (tw_c * sum_s - tw_s * sum_c).astype(jnp.bfloat16)

    transform(0)
    for t in range(K // KT):
        if t + 1 < K // KT:
            transform(t + 1)
        twist(t)
    for here in (slice(0, half), slice(half, total)):
        result[here] = jnp.dot(spread[here], table_t[...], preferred_element_type=jnp.float32)


def wrapped(index, count):
    return jnp.where(index >= count, index - count, index)


def shift_rows(cells, down, edge):
    row = lax.broadcasted_iota(jnp.int32, cells.shape, 0)
    last = cells.shape[0] - 1
    if down:
        return jnp.where(row == 0, edge, pltpu.roll(cells, 1, 0))
    return jnp.where(row == last, edge, pltpu.roll(cells, last, 0))


def shift_cols(cells, right, edge):
    lane = lax.broadcasted_iota(jnp.int32, cells.shape, 1)
    last = cells.shape[1] - 1
    if right:
        return jnp.where(lane == 0, edge, pltpu.roll(cells, 1, 1))
    return jnp.where(lane == last, edge, pltpu.roll(cells, last, 1))


def window_kernel(
    n_ref, nu_hbm, src_hbm, dst_hbm, live_hbm, force_hbm, mix_hbm, mask_hbm, weight_hbm, u_hbm, v_hbm,
    out_ocean, out_u, out_v,
    nu_ref, src_ref, dst_ref, live_ref, force, mix, mask, weight, last_u, load_sem,
    cells, ratio, ocean, send_n, send_s, send_w, send_e, got_n, got_s, got_w, got_e, halo_send, halo_recv,
    flux, note, notes, note_send, note_recv,
    stage, got_v, got_even, got_odd, fwd_send, fwd_recv,
    coarse, fine, coarse_t, fine_t, table, table_t, twiddle,
    packed, raw, spread, result, back_v, back_even, back_odd, blank, back_send, back_recv, ocean_sem,
):
    me, oc = lax.axis_index("lon"), lax.axis_index("ocn")
    n_lon, n_ocn = lax.axis_size("lon"), lax.axis_size("ocn")
    levels = cells.shape[0] - 1
    last_owner = n_lon - 1
    share = 2
    source = me < NBLK
    start_at = wrapped(me, NBLK)

    def mine(t):
        return pl.ds(share * t, share)

    loads = [
        pltpu.make_async_copy(force_hbm, force, load_sem.at[0]),
        pltpu.make_async_copy(mix_hbm, mix, load_sem.at[1]),
        pltpu.make_async_copy(mask_hbm, mask, load_sem.at[2]),
        pltpu.make_async_copy(weight_hbm.at[pl.ds(0, NBLK)], weight, load_sem.at[3]),
        pltpu.make_async_copy(u_hbm.at[pl.ds(share * n_lon - 1, 1)], last_u, load_sem.at[4]),
        pltpu.make_async_copy(nu_hbm, nu_ref, load_sem.at[5]),
        pltpu.make_async_copy(src_hbm, src_ref, load_sem.at[6]),
        pltpu.make_async_copy(dst_hbm, dst_ref, load_sem.at[7]),
        pltpu.make_async_copy(live_hbm, live_ref, load_sem.at[8]),
    ]
    for load in loads:
        load.start()

    barrier = pltpu.get_barrier_semaphore()

    def greet(i, carry):
        pl.semaphore_signal(barrier, inc=1, device_id={"lon": wrapped(me + i, n_lon)}, device_id_type=MESH)
        return carry

    lax.fori_loop(1, n_lon, greet, 0)

    @pl.when(oc > 0)
    def _():
        pl.semaphore_signal(barrier, inc=1, device_id={"ocn": oc - 1}, device_id_type=MESH)

    @pl.when(oc < n_ocn - 1)
    def _():
        pl.semaphore_signal(barrier, inc=1, device_id={"ocn": oc + 1}, device_id_type=MESH)

    points = n_ref[0].astype(jnp.float32)
    build_tables(points, coarse, fine, coarse_t, fine_t, table, table_t, twiddle)

    for load in loads[:3]:
        load.wait()
    zero = jnp.zeros(force.shape[1:], jnp.float32)
    rat, val, below = zero, zero, zero
    for z in range(levels - 1, -1, -1):
        above = mix[z - 1] if z > 0 else zero
        inv = 1.0 / (1.0 + above + below * (1.0 - rat))
        val = (force[z] + below * val) * inv
        rat = above * inv
        cells[z] = val
        ratio[z] = rat
        below = above
    lane = lax.broadcasted_iota(jnp.int32, zero.shape, 1)
    west, east = zero, zero
    send_n[pl.ds(levels, 8), :] = zero
    send_s[pl.ds(levels, 8), :] = zero
    s = zero
    for z in range(levels + 1):
        if z < levels:
            s = cells[z] + ratio[z] * s if z > 0 else cells[0]
        else:
            s = mask[...].astype(jnp.float32)
        cells[z] = s
        send_n[z : z + 1, :] = s[0:1, :]
        send_s[z : z + 1, :] = s[7:8, :]
        west = jnp.where(lane == z, jnp.broadcast_to(s[:, 0:1], s.shape), west)
        east = jnp.where(lane == z, jnp.broadcast_to(s[:, BLK - 1 : BLK], s.shape), east)
    send_w[...] = west
    send_e[...] = east

    pl.semaphore_wait(barrier, n_lon - 1 + (oc > 0).astype(jnp.int32) + (oc < n_ocn - 1).astype(jnp.int32))

    sides = (
        (oc > 0, oc < n_ocn - 1, {"ocn": oc - 1}, send_n, got_s),
        (oc < n_ocn - 1, oc > 0, {"ocn": oc + 1}, send_s, got_n),
        (me > 0, me < n_lon - 1, {"lon": me - 1}, send_w, got_e),
        (me < n_lon - 1, me > 0, {"lon": me + 1}, send_e, got_w),
    )

    def halo(i):
        has, gets, where, out, into = sides[i]
        return has, gets, into, pltpu.make_async_remote_copy(
            src_ref=out, dst_ref=into, send_sem=halo_send.at[i], recv_sem=halo_recv.at[i], device_id=where, device_id_type=MESH
        )

    for i in range(4):
        has, gets, into, copy = halo(i)
        pl.when(has)(copy.start)

        @pl.when(jnp.logical_not(gets))
        def _(into=into):
            into[...] = jnp.zeros_like(into)

    groups = (
        (v_hbm, 0, 2, got_v, back_v, out_v, 0),
        (u_hbm, 0, 1, got_even, back_even, out_u, 1),
        (u_hbm, 1, 1, got_odd, back_odd, out_u, 1),
    )

    def send_rows(g):
        field, first, depth, got = groups[g][:4]

        def rows_of(t):
            return field.at[pl.ds(share * t + first, depth)]

        def forward(i, carry):
            t = wrapped(me + i, n_lon)

            def start():
                pltpu.make_async_remote_copy(
                    src_ref=rows_of(t), dst_ref=got.at[me], send_sem=fwd_send.at[g], recv_sem=fwd_recv.at[g], device_id={"lon": t}, device_id_type=MESH
                ).start()

            if g < 2:
                start()
            else:
                pl.when(t != last_owner)(start)
            return carry

        lax.fori_loop(1, n_lon, forward, 0, unroll=4)
        pltpu.make_async_copy(rows_of(me), got.at[me], fwd_recv.at[g]).start()

    @pl.when(source)
    def _():
        for g in range(2):
            send_rows(g)

    for i in range(4):
        has, gets, into, copy = halo(i)
        pl.when(gets)(copy.wait_recv)
        pl.when(has)(copy.wait_send)

    m = cells[levels]
    m_n, m_s = shift_rows(m, True, got_n[levels : levels + 1, :]), shift_rows(m, False, got_s[levels : levels + 1, :])
    m_w = shift_cols(m, True, jnp.broadcast_to(got_w[:, levels : levels + 1], m.shape))
    m_e = shift_cols(m, False, jnp.broadcast_to(got_e[:, levels : levels + 1], m.shape))

    def mixed(z):
        s = cells[z]
        near = m_n * (shift_rows(s, True, got_n[z : z + 1, :]) - s)
        near += m_s * (shift_rows(s, False, got_s[z : z + 1, :]) - s)
        near += m_w * (shift_cols(s, True, jnp.broadcast_to(got_w[:, z : z + 1], s.shape)) - s)
        near += m_e * (shift_cols(s, False, jnp.broadcast_to(got_e[:, z : z + 1], s.shape)) - s)
        return m * (s + NU_MIX * near)

    surface = mixed(0)
    ocean[0] = surface
    flux[...] = surface.astype(jnp.bfloat16).astype(jnp.float32)
    for load in loads[3:4] + loads[6:]:
        load.wait()

    def owner(p, carry):
        one = flux[pl.ds(src_ref[0, p], 1), :]
        two = flux[pl.ds(src_ref[1, p], 1), :]
        row = lax.broadcasted_iota(jnp.int32, (8, BLK), 0)
        lhs = jnp.concatenate([jnp.where(row == 0, one, 0.0), jnp.where(row == 1, two, 0.0)], 1).astype(jnp.bfloat16)
        both = jnp.concatenate([weight[p, 0], weight[p, 1]], 1)
        got = lax.dot_general(lhs, both, (((1,), (1,)), ((), ())), preferred_element_type=jnp.float32)
        code_0 = live_ref[0, p] * (dst_ref[0, p] + 1) - 1
        code_1 = live_ref[1, p] * (dst_ref[1, p] + 1) - 1
        codes = jnp.where(row == 2, code_0, code_1).astype(jnp.float32)
        note[p] = jnp.where(row < 2, got, codes)[0:4]
        return carry

    lax.fori_loop(0, NBLK, owner, 0, unroll=21)

    def tell(i, carry):
        p = wrapped(start_at + i, NBLK)

        @pl.when(p != me)
        def _():
            pltpu.make_async_remote_copy(
                src_ref=note.at[p], dst_ref=notes.at[me], send_sem=note_send, recv_sem=note_recv, device_id={"lon": p}, device_id_type=MESH
            ).start()

        return carry

    lax.fori_loop(0, NBLK, tell, 0, unroll=3)

    @pl.when(source)
    def _():
        pltpu.make_async_copy(note.at[me], notes.at[me], note_recv).start()
        send_rows(2)

    for z in range(1, levels):
        ocean[z] = mixed(z)
    ocean_copy = pltpu.make_async_copy(ocean, out_ocean, ocean_sem)
    ocean_copy.start()
    loads[4].wait()

    def couple():
        pltpu.make_async_copy(notes, notes, note_recv).wait()
        even = 2.0 * iota((8, BLK), 0)
        odd = even + 1.0

        def add(l, sums):
            sum_even, sum_odd = sums
            block = notes[l]
            for c in range(2):
                value, code = block[c : c + 1, :], block[c + 2 : c + 3, :]
                sum_even += jnp.where(code == even, value, 0.0)
                sum_odd += jnp.where(code == odd, value, 0.0)
            return sum_even, sum_odd

        blank_sum = jnp.zeros((8, BLK), jnp.float32)
        sum_even, sum_odd = lax.fori_loop(0, n_lon, add, (blank_sum, blank_sum), unroll=4)
        coupling = jnp.concatenate([sum_even, sum_odd], 1)
        stage[0] = (last_u[0].astype(jnp.float32) + coupling).astype(jnp.bfloat16)
        pltpu.make_async_remote_copy(
            src_ref=stage, dst_ref=got_odd.at[me], send_sem=fwd_send.at[2], recv_sem=fwd_recv.at[2], device_id={"lon": last_owner}, device_id_type=MESH
        ).start()

    loads[5].wait()
    for g, (field, first, depth, got, back, out, f) in enumerate(groups):
        rows = 8 * depth
        column = iota((rows, SEGLON), 1)
        if g == 1:
            pl.when(source)(couple)
        pltpu.make_async_copy(got, got, fwd_recv.at[g]).wait()

        def pack(l, carry, got=got, rows=rows, column=column):
            inside = column + (l * SEGLON).astype(jnp.float32) < points
            block = got[l].astype(jnp.float32).reshape(rows, SEGLON)
            result[pl.ds(pl.multiple_of(rows * l, 8), rows), :] = jnp.where(inside, block, 0.0)
            return carry

        lax.fori_loop(0, NBLK, pack, 0, unroll=3)
        total = pl.ds(0, NBLK * rows)
        packed[total, :] = result[total, :].astype(jnp.bfloat16)
        viscosity = nu_ref[share * me + first]
        if depth == 2:
            viscosity = jnp.where(lax.broadcasted_iota(jnp.int32, (rows, KT), 0) < 8, viscosity, nu_ref[share * me + 1])
        spectral(rows, points, viscosity, packed, table, table_t, twiddle, raw, spread, result)
        own = pl.ds(share * me + first, depth)

        def unpack(i, carry, back=back, out=out, rows=rows, depth=depth, column=column, own=own, g=g, f=f):
            l = wrapped(start_at + i, NBLK)
            inside = column + (l * SEGLON).astype(jnp.float32) < points
            block = result[pl.ds(pl.multiple_of(rows * l, 8), rows), :]
            back[l] = jnp.where(inside, block, 0.0).reshape(depth, 8, SEGLON).astype(jnp.bfloat16)

            @pl.when(l != me)
            def _():
                pltpu.make_async_remote_copy(
                    src_ref=back.at[l], dst_ref=out.at[own], send_sem=back_send.at[g], recv_sem=back_recv.at[f], device_id={"lon": l}, device_id_type=MESH
                ).start()

            return carry

        lax.fori_loop(0, NBLK, unpack, 0, unroll=3)

        @pl.when(source)
        def _(back=back, out=out, own=own, f=f):
            pltpu.make_async_copy(back.at[me], out.at[own], back_recv.at[f]).start()

        @pl.when(jnp.logical_not(source))
        def _(out=out, g=g, f=f):
            if g == 0:
                blank[...] = jnp.zeros_like(blank)
            if g < 2:
                pltpu.make_async_copy(blank, out, back_recv.at[f]).start()

    ocean_copy.wait()

    @pl.when(source)
    def _():
        for g, (field, first, depth, got, back, out, f) in enumerate(groups):
            sent = field.at[pl.ds(0, depth * (n_lon - 1))]
            pltpu.make_async_copy(sent, sent, fwd_send.at[g]).wait()
        told = note.at[pl.ds(0, NBLK - 1)]
        pltpu.make_async_copy(told, told, note_send).wait()

    @pl.when(jnp.logical_not(source))
    def _():
        pltpu.make_async_copy(note, note, note_send).wait()

    for g, (field, first, depth, got, back, out, f) in enumerate(groups):

        @pl.when(source)
        def _(back=back, g=g):
            sent = back.at[pl.ds(0, NBLK - 1)]
            pltpu.make_async_copy(sent, sent, back_send.at[g]).wait()

        @pl.when(jnp.logical_not(source))
        def _(back=back, g=g):
            pltpu.make_async_copy(back, back, back_send.at[g]).wait()

    for f, out in enumerate((out_v, out_u)):
        pltpu.make_async_copy(out, out, back_recv.at[f]).wait()


def finish_kernel(ocean_in, u_in, v_in, ocean_out, u_out, v_out, sems):
    pairs = ((ocean_in, ocean_out), (u_in, u_out), (v_in, v_out))
    copies = [pltpu.make_async_copy(here, there, sems.at[i]) for i, (here, there) in enumerate(pairs)]
    for copy in copies:
        copy.start()
    for copy in copies:
        copy.wait()


def per_device(
    ocean_adjoint,
    mixing_coef,
    land_mask,
    remap_src,
    remap_dst,
    remap_live,
    remap_weight,
    atm_u,
    atm_v,
    spectral_nu,
    band_points,
):
    lon_devices = lax.axis_size("lon")
    levels = ocean_adjoint.shape[0]
    slots = remap_src.shape[2:]
    tile = ocean_adjoint.shape[1:]
    m = 16 * NBLK
    f32, bf16, dma = jnp.float32, jnp.bfloat16, pltpu.SemaphoreType.DMA
    smem = pl.BlockSpec(memory_space=pltpu.SMEM)
    hbm = pl.BlockSpec(memory_space=pltpu.HBM)
    anywhere = pl.BlockSpec(memory_space=pl.ANY)
    one = (1,) + atm_u.shape[1:]
    two = (2,) + atm_u.shape[1:]
    edge = (levels + 8, BLK)
    shapes = (
        jax.ShapeDtypeStruct(ocean_adjoint.shape, f32),
        jax.ShapeDtypeStruct(atm_u.shape, bf16),
        jax.ShapeDtypeStruct(atm_v.shape, bf16),
    )
    results = pl.pallas_call(
        window_kernel,
        out_shape=tuple(pltpu.VMEM(x.shape, x.dtype) for x in shapes),
        in_specs=[smem] + [hbm] * 10,
        out_specs=(anywhere, anywhere, anywhere),
        scratch_shapes=[
            pltpu.SMEM(spectral_nu.shape, f32),
            pltpu.SMEM(slots[::-1], jnp.int32),
            pltpu.SMEM(slots[::-1], jnp.int32),
            pltpu.SMEM(slots[::-1], jnp.int32),
            pltpu.VMEM(ocean_adjoint.shape, f32),
            pltpu.VMEM(mixing_coef.shape, f32),
            pltpu.VMEM(land_mask.shape, jnp.int32),
            pltpu.VMEM((NBLK, slots[1], BLK, BLK), bf16),
            pltpu.VMEM(one, bf16),
            dma((9,)),
            pltpu.VMEM((levels + 1,) + tile, f32),
            pltpu.VMEM((levels,) + tile, f32),
            pltpu.VMEM((levels,) + tile, f32),
            pltpu.VMEM(edge, f32),
            pltpu.VMEM(edge, f32),
            pltpu.VMEM(tile, f32),
            pltpu.VMEM(tile, f32),
            pltpu.VMEM(edge, f32),
            pltpu.VMEM(edge, f32),
            pltpu.VMEM(tile, f32),
            pltpu.VMEM(tile, f32),
            dma((4,)),
            dma((4,)),
            pltpu.VMEM(tile, f32),
            pltpu.VMEM((NBLK, 4, BLK), f32),
            pltpu.VMEM((lon_devices, 4, BLK), f32),
            dma,
            dma,
            pltpu.VMEM(one, bf16),
            pltpu.VMEM((NBLK,) + two, bf16),
            pltpu.VMEM((NBLK,) + one, bf16),
            pltpu.VMEM((NBLK,) + one, bf16),
            dma((3,)),
            dma((3,)),
            pltpu.VMEM((2, 16, K), f32),
            pltpu.VMEM((2, 16, K), f32),
            pltpu.VMEM((2, K // 16, SEGLON), f32),
            pltpu.VMEM((2, 16, SEGLON), f32),
            pltpu.VMEM((SEGLON, 2 * K), bf16),
            pltpu.VMEM((2 * K, SEGLON), bf16),
            pltpu.VMEM((2, TWROWS, K), f32),
            pltpu.VMEM((m, SEGLON), bf16),
            pltpu.VMEM((K // KT, 2, m, KT), f32),
            pltpu.VMEM((m, 2 * K), bf16),
            pltpu.VMEM((m, SEGLON), f32),
            pltpu.VMEM((NBLK,) + two, bf16),
            pltpu.VMEM((NBLK,) + one, bf16),
            pltpu.VMEM((NBLK,) + one, bf16),
            pltpu.VMEM(atm_u.shape, bf16),
            dma((3,)),
            dma((2,)),
            dma,
        ],
        compiler_params=pltpu.CompilerParams(collective_id=0, has_side_effects=True),
        name="window",
    )(
        band_points,
        spectral_nu,
        remap_src.reshape(slots).T,
        remap_dst.reshape(slots).T,
        remap_live.reshape(slots).T,
        ocean_adjoint,
        mixing_coef,
        land_mask,
        remap_weight.reshape(remap_weight.shape[2:]),
        atm_u,
        atm_v,
    )
    return pl.pallas_call(
        finish_kernel,
        out_shape=shapes,
        in_specs=[pl.BlockSpec(memory_space=pltpu.VMEM)] * 3,
        out_specs=(hbm, hbm, hbm),
        scratch_shapes=[dma((3,))],
        compiler_params=pltpu.CompilerParams(vmem_limit_bytes=8 << 20),
        name="finish",
    )(*results)


def solution(mesh):
    placed = (
        P(None, "ocn", "lon"),
        P(None, "ocn", "lon"),
        P("ocn", "lon"),
        P("ocn", "lon", None, None),
        P("ocn", "lon", None, None),
        P("ocn", "lon", None, None),
        P("ocn", "lon", None, None, None, None),
        P(None, "ocn", "lon"),
        P(None, "ocn", "lon"),
        P(),
        P("ocn"),
    )
    return jax.shard_map(
        per_device,
        mesh=mesh,
        in_specs=placed,
        out_specs=(P(None, "ocn", "lon"), P(None, "ocn", "lon"), P(None, "ocn", "lon")),
        check_vma=False,
    )
```

```python
import math

import jax
import jax.numpy as jnp
from jax import lax
from jax.experimental import pallas as pl
from jax.experimental.pallas import tpu as pltpu
from jax.sharding import PartitionSpec as P

K = 1280
BLK = 128
SEGLON = 256
NBLK = 21
TWROWS = 24
KT = 256
NU_MIX = 0.2
MESH = pl.DeviceIdType.MESH

COS_C = [(-1.0) ** m * (2.0 * math.pi) ** (2 * m) / math.factorial(2 * m) for m in range(11)]
SIN_C = [(-1.0) ** m * (2.0 * math.pi) ** (2 * m + 1) / math.factorial(2 * m + 1) for m in range(11)]


def iota(shape, dim):
    return lax.broadcasted_iota(jnp.int32, shape, dim).astype(jnp.float32)


def cos_sin(steps, points):
    inverse = 1.0 / points
    turns = jnp.floor(steps * inverse + 0.5)
    part = (steps - turns * points) * inverse
    square = part * part
    cosine = jnp.full_like(square, COS_C[10])
    sine = jnp.full_like(square, SIN_C[10])
    for m in range(9, -1, -1):
        cosine = cosine * square + COS_C[m]
        sine = sine * square + SIN_C[m]
    return cosine, sine * part


def build_tables(points, coarse, fine, coarse_t, fine_t, table, table_t, twiddle):
    n_row = jnp.full((16, K), points, jnp.float32)
    step_row, wave_row = iota((16, K), 0), iota((16, K), 1)
    coarse[0], coarse[1] = cos_sin(16.0 * step_row * wave_row, n_row)
    fine[0], fine[1] = cos_sin(step_row * wave_row, n_row)
    n_tw = jnp.full((TWROWS, K), points, jnp.float32)
    twiddle[0], twiddle[1] = cos_sin(float(SEGLON) * iota((TWROWS, K), 0) * iota((TWROWS, K), 1), n_tw)
    n_t = jnp.full((K // 16, SEGLON), points, jnp.float32)
    coarse_t[0], coarse_t[1] = cos_sin(16.0 * iota((K // 16, SEGLON), 0) * iota((K // 16, SEGLON), 1), n_t)
    n_f = jnp.full((16, SEGLON), points, jnp.float32)
    fine_t[0], fine_t[1] = cos_sin(iota((16, SEGLON), 0) * iota((16, SEGLON), 1), n_f)

    def rows(p, carry):
        cos_p, sin_p = coarse[0, pl.ds(p, 1), :], coarse[1, pl.ds(p, 1), :]
        here = pl.ds(pl.multiple_of(16 * p, 16), 16)
        table[here, 0:K] = (cos_p * fine[0] - sin_p * fine[1]).astype(jnp.bfloat16)
        table[here, K : 2 * K] = (sin_p * fine[0] + cos_p * fine[1]).astype(jnp.bfloat16)
        return carry

    lax.fori_loop(0, SEGLON // 16, rows, 0)

    def rows_t(p, carry):
        cos_p, sin_p = coarse_t[0, pl.ds(p, 1), :], coarse_t[1, pl.ds(p, 1), :]
        here = pl.ds(pl.multiple_of(16 * p, 16), 16)
        table_t[here, :] = (cos_p * fine_t[0] - sin_p * fine_t[1]).astype(jnp.bfloat16)
        table_t[pl.ds(pl.multiple_of(K + 16 * p, 16), 16), :] = (sin_p * fine_t[0] + cos_p * fine_t[1]).astype(jnp.bfloat16)
        return carry

    lax.fori_loop(0, K // 16, rows_t, 0, unroll=2)


def spectral(rows, points, viscosity, packed, table, table_t, twiddle, raw, spread, result):
    total = NBLK * rows
    half = (total // 2 + 15) // 16 * 16
    scale = 2.0 / jnp.full((rows, KT), points, jnp.float32)

    def transform(t):
        for part in range(2):
            at = part * K + t * KT
            raw[t, part, 0:total, :] = jnp.dot(packed[0:total, :], table[:, at : at + KT], preferred_element_type=jnp.float32)

    def twist(t):
        cos_at, sin_at = slice(t * KT, (t + 1) * KT), slice(K + t * KT, K + (t + 1) * KT)
        sum_c = jnp.zeros((rows, KT), jnp.float32)
        sum_s = jnp.zeros((rows, KT), jnp.float32)
        for l in range(NBLK):
            here = slice(l * rows, (l + 1) * rows)
            part_c, part_s = raw[t, 0, here, :], raw[t, 1, here, :]
            tw_c, tw_s = twiddle[0, l : l + 1, cos_at], twiddle[1, l : l + 1, cos_at]
            sum_c += tw_c * part_c - tw_s * part_s
            sum_s += tw_s * part_c + tw_c * part_s
        ratio = (iota((rows, KT), 1) + float(t * KT)) * (1.0 / K)
        damping = scale / (1.0 + viscosity * ratio * ratio)
        sum_c *= damping
        sum_s *= damping
        for l in range(NBLK):
            here = slice(l * rows, (l + 1) * rows)
            tw_c, tw_s = twiddle[0, l : l + 1, cos_at], twiddle[1, l : l + 1, cos_at]
            spread[here, cos_at] = (tw_c * sum_c + tw_s * sum_s).astype(jnp.bfloat16)
            spread[here, sin_at] = (tw_c * sum_s - tw_s * sum_c).astype(jnp.bfloat16)

    transform(0)
    for t in range(K // KT):
        if t + 1 < K // KT:
            transform(t + 1)
        twist(t)
    for here in (slice(0, half), slice(half, total)):
        result[here] = jnp.dot(spread[here], table_t[...], preferred_element_type=jnp.float32)


STEPS = [((2, 1, 3, 0)[(a + b) % 4], (2, 1, 3, 0)[b], core) for a in range(4) for b in range(4) for core in range(2)]


def wrapped(index, count):
    return jnp.where(index >= count, index - count, index)


def shift_rows(cells, down, edge):
    row = lax.broadcasted_iota(jnp.int32, cells.shape, 0)
    last = cells.shape[0] - 1
    if down:
        return jnp.where(row == 0, edge, pltpu.roll(cells, 1, 0))
    return jnp.where(row == last, edge, pltpu.roll(cells, last, 0))


def shift_cols(cells, right, edge):
    lane = lax.broadcasted_iota(jnp.int32, cells.shape, 1)
    last = cells.shape[1] - 1
    if right:
        return jnp.where(lane == 0, edge, pltpu.roll(cells, 1, 1))
    return jnp.where(lane == last, edge, pltpu.roll(cells, last, 1))


def window_kernel(
    n_ref, nu_hbm, src_hbm, dst_hbm, live_hbm, force_hbm, mix_hbm, mask_hbm, weight_hbm, u_hbm, v_hbm,
    out_ocean, out_u, out_v,
    nu_ref, src_ref, dst_ref, live_ref, force, mix, mask, weight, last_u, load_sem,
    cells, ratio, ocean, send_n, send_s, send_w, send_e, got_n, got_s, got_w, got_e, halo_send, halo_recv,
    flux, note, notes, note_send, note_recv,
    stage, got_v, got_even, got_odd, fwd_send, fwd_recv,
    coarse, fine, coarse_t, fine_t, table, table_t, twiddle,
    packed, raw, spread, result, back_v, back_even, back_odd, blank, back_send, back_recv, ocean_sem,
):
    me, oc = lax.axis_index("lon"), lax.axis_index("ocn")
    n_lon, n_ocn = lax.axis_size("lon"), lax.axis_size("ocn")
    levels = cells.shape[0] - 1
    last_owner = n_lon - 1
    share = 2
    source = me < NBLK
    start_at = wrapped(me, NBLK)
    x, y, core = me // 8, lax.rem(me // 2, 4), lax.rem(me, 2)
    x_at = [8 * wrapped(x + d, 4) for d in range(4)]
    y_at = [2 * wrapped(y + d, 4) for d in range(4)]
    c_at = [core, 1 - core]

    def peer(step):
        return x_at[step[0]] + y_at[step[1]] + c_at[step[2]]


    def mine(t):
        return pl.ds(share * t, share)

    loads = [
        pltpu.make_async_copy(force_hbm, force, load_sem.at[0]),
        pltpu.make_async_copy(mix_hbm, mix, load_sem.at[1]),
        pltpu.make_async_copy(mask_hbm, mask, load_sem.at[2]),
        pltpu.make_async_copy(weight_hbm.at[pl.ds(0, NBLK)], weight, load_sem.at[3]),
        pltpu.make_async_copy(u_hbm.at[pl.ds(share * n_lon - 1, 1)], last_u, load_sem.at[4]),
        pltpu.make_async_copy(nu_hbm, nu_ref, load_sem.at[5]),
        pltpu.make_async_copy(src_hbm, src_ref, load_sem.at[6]),
        pltpu.make_async_copy(dst_hbm, dst_ref, load_sem.at[7]),
        pltpu.make_async_copy(live_hbm, live_ref, load_sem.at[8]),
    ]
    barrier = pltpu.get_barrier_semaphore()
    for step in STEPS:
        if step != (0, 0, 0):
            pl.semaphore_signal(barrier, inc=1, device_id={"lon": peer(step)}, device_id_type=MESH)

    @pl.when(oc > 0)
    def _():
        pl.semaphore_signal(barrier, inc=1, device_id={"ocn": oc - 1}, device_id_type=MESH)

    @pl.when(oc < n_ocn - 1)
    def _():
        pl.semaphore_signal(barrier, inc=1, device_id={"ocn": oc + 1}, device_id_type=MESH)

    for load in loads:
        load.start()

    for load in loads[:3]:
        load.wait()
    zero = jnp.zeros(force.shape[1:], jnp.float32)
    rat, val, below = zero, zero, zero
    for z in range(levels - 1, -1, -1):
        above = mix[z - 1] if z > 0 else zero
        inv = 1.0 / (1.0 + above + below * (1.0 - rat))
        val = (force[z] + below * val) * inv
        rat = above * inv
        cells[z] = val
        ratio[z] = rat
        below = above
    lane = lax.broadcasted_iota(jnp.int32, zero.shape, 1)
    west, east = zero, zero
    send_n[pl.ds(levels, 8), :] = zero
    send_s[pl.ds(levels, 8), :] = zero
    s = zero
    for z in range(levels + 1):
        if z < levels:
            s = cells[z] + ratio[z] * s if z > 0 else cells[0]
        else:
            s = mask[...].astype(jnp.float32)
        cells[z] = s
        send_n[z : z + 1, :] = s[0:1, :]
        send_s[z : z + 1, :] = s[7:8, :]
        west = jnp.where(lane == z, jnp.broadcast_to(s[:, 0:1], s.shape), west)
        east = jnp.where(lane == z, jnp.broadcast_to(s[:, BLK - 1 : BLK], s.shape), east)
    send_w[...] = west
    send_e[...] = east

    pl.semaphore_wait(barrier, n_lon - 1 + (oc > 0).astype(jnp.int32) + (oc < n_ocn - 1).astype(jnp.int32))

    sides = (
        (oc > 0, oc < n_ocn - 1, {"ocn": oc - 1}, send_n, got_s),
        (oc < n_ocn - 1, oc > 0, {"ocn": oc + 1}, send_s, got_n),
        (me > 0, me < n_lon - 1, {"lon": me - 1}, send_w, got_e),
        (me < n_lon - 1, me > 0, {"lon": me + 1}, send_e, got_w),
    )

    def halo(i):
        has, gets, where, out, into = sides[i]
        return has, gets, into, pltpu.make_async_remote_copy(
            src_ref=out, dst_ref=into, send_sem=halo_send.at[i], recv_sem=halo_recv.at[i], device_id=where, device_id_type=MESH
        )

    for i in range(4):
        has, gets, into, copy = halo(i)
        pl.when(has)(copy.start)

        @pl.when(jnp.logical_not(gets))
        def _(into=into):
            into[...] = jnp.zeros_like(into)

    groups = (
        (v_hbm, 0, 2, got_v, back_v, out_v, 0),
        (u_hbm, 0, 1, got_even, back_even, out_u, 1),
        (u_hbm, 1, 1, got_odd, back_odd, out_u, 1),
    )

    def send_rows(g):
        field, first, depth, got = groups[g][:4]

        def rows_of(t):
            return field.at[pl.ds(share * t + first, depth)]

        for step in STEPS:
            if step == (0, 0, 0):
                continue
            t = peer(step)
            copy = pltpu.make_async_remote_copy(
                src_ref=rows_of(t), dst_ref=got.at[me], send_sem=fwd_send.at[g], recv_sem=fwd_recv.at[g], device_id={"lon": t}, device_id_type=MESH
            )
            if g < 2:
                copy.start()
            else:
                pl.when(t != last_owner)(copy.start)

        pltpu.make_async_copy(rows_of(me), got.at[me], fwd_recv.at[g]).start()

    @pl.when(source)
    def _():
        for g in range(2):
            send_rows(g)

    points = n_ref[0].astype(jnp.float32)
    build_tables(points, coarse, fine, coarse_t, fine_t, table, table_t, twiddle)

    for i in range(4):
        has, gets, into, copy = halo(i)
        pl.when(gets)(copy.wait_recv)
        pl.when(has)(copy.wait_send)

    m = cells[levels]
    m_n, m_s = shift_rows(m, True, got_n[levels : levels + 1, :]), shift_rows(m, False, got_s[levels : levels + 1, :])
    m_w = shift_cols(m, True, jnp.broadcast_to(got_w[:, levels : levels + 1], m.shape))
    m_e = shift_cols(m, False, jnp.broadcast_to(got_e[:, levels : levels + 1], m.shape))

    def mixed(z):
        s = cells[z]
        near = m_n * (shift_rows(s, True, got_n[z : z + 1, :]) - s)
        near += m_s * (shift_rows(s, False, got_s[z : z + 1, :]) - s)
        near += m_w * (shift_cols(s, True, jnp.broadcast_to(got_w[:, z : z + 1], s.shape)) - s)
        near += m_e * (shift_cols(s, False, jnp.broadcast_to(got_e[:, z : z + 1], s.shape)) - s)
        return m * (s + NU_MIX * near)

    surface = mixed(0)
    ocean[0] = surface
    flux[...] = surface.astype(jnp.bfloat16).astype(jnp.float32)
    for load in loads[3:4] + loads[6:]:
        load.wait()

    def owner(p, carry):
        one = flux[pl.ds(src_ref[0, p], 1), :]
        two = flux[pl.ds(src_ref[1, p], 1), :]
        row = lax.broadcasted_iota(jnp.int32, (8, BLK), 0)
        lhs = jnp.concatenate([jnp.where(row == 0, one, 0.0), jnp.where(row == 1, two, 0.0)], 1).astype(jnp.bfloat16)
        both = jnp.concatenate([weight[p, 0], weight[p, 1]], 1)
        got = lax.dot_general(lhs, both, (((1,), (1,)), ((), ())), preferred_element_type=jnp.float32)
        code_0 = live_ref[0, p] * (dst_ref[0, p] + 1) - 1
        code_1 = live_ref[1, p] * (dst_ref[1, p] + 1) - 1
        codes = jnp.where(row == 2, code_0, code_1).astype(jnp.float32)
        note[p] = jnp.where(row < 2, got, codes)[0:4]
        return carry

    lax.fori_loop(0, NBLK, owner, 0, unroll=21)

    def tell(i, carry):
        p = wrapped(start_at + i, NBLK)

        @pl.when(p != me)
        def _():
            pltpu.make_async_remote_copy(
                src_ref=note.at[p], dst_ref=notes.at[me], send_sem=note_send, recv_sem=note_recv, device_id={"lon": p}, device_id_type=MESH
            ).start()

        return carry

    lax.fori_loop(0, NBLK, tell, 0, unroll=3)

    @pl.when(source)
    def _():
        pltpu.make_async_copy(note.at[me], notes.at[me], note_recv).start()
        send_rows(2)

    for z in range(1, levels):
        ocean[z] = mixed(z)
    ocean_copy = pltpu.make_async_copy(ocean, out_ocean, ocean_sem)
    ocean_copy.start()
    loads[4].wait()

    def couple():
        pltpu.make_async_copy(notes, notes, note_recv).wait()
        even = 2.0 * iota((8, BLK), 0)
        odd = even + 1.0

        def add(l, sums):
            sum_even, sum_odd = sums
            block = notes[l]
            for c in range(2):
                value, code = block[c : c + 1, :], block[c + 2 : c + 3, :]
                sum_even += jnp.where(code == even, value, 0.0)
                sum_odd += jnp.where(code == odd, value, 0.0)
            return sum_even, sum_odd

        blank_sum = jnp.zeros((8, BLK), jnp.float32)
        sum_even, sum_odd = lax.fori_loop(0, n_lon, add, (blank_sum, blank_sum), unroll=4)
        coupling = jnp.concatenate([sum_even, sum_odd], 1)
        stage[0] = (last_u[0].astype(jnp.float32) + coupling).astype(jnp.bfloat16)
        pltpu.make_async_remote_copy(
            src_ref=stage, dst_ref=got_odd.at[me], send_sem=fwd_send.at[2], recv_sem=fwd_recv.at[2], device_id={"lon": last_owner}, device_id_type=MESH
        ).start()

    loads[5].wait()
    for g, (field, first, depth, got, back, out, f) in enumerate(groups):
        rows = 8 * depth
        column = iota((rows, SEGLON), 1)
        if g == 1:
            pl.when(source)(couple)
        pltpu.make_async_copy(got, got, fwd_recv.at[g]).wait()

        def pack(l, carry, got=got, rows=rows, column=column):
            inside = column + (l * SEGLON).astype(jnp.float32) < points
            block = got[l].astype(jnp.float32).reshape(rows, SEGLON)
            result[pl.ds(pl.multiple_of(rows * l, 8), rows), :] = jnp.where(inside, block, 0.0)
            return carry

        lax.fori_loop(0, NBLK, pack, 0, unroll=3)
        total = pl.ds(0, NBLK * rows)
        packed[total, :] = result[total, :].astype(jnp.bfloat16)
        viscosity = nu_ref[share * me + first]
        if depth == 2:
            viscosity = jnp.where(lax.broadcasted_iota(jnp.int32, (rows, KT), 0) < 8, viscosity, nu_ref[share * me + 1])
        spectral(rows, points, viscosity, packed, table, table_t, twiddle, raw, spread, result)
        own = pl.ds(share * me + first, depth)

        def unpack(l, carry, back=back, rows=rows, depth=depth, column=column):
            inside = column + (l * SEGLON).astype(jnp.float32) < points
            block = result[pl.ds(pl.multiple_of(rows * l, 8), rows), :]
            back[l] = jnp.where(inside, block, 0.0).reshape(depth, 8, SEGLON).astype(jnp.bfloat16)
            return carry

        lax.fori_loop(0, NBLK, unpack, 0, unroll=7)
        for step in STEPS:
            if step == (0, 0, 0):
                continue
            l = peer(step)

            @pl.when(l < NBLK)
            def _(l=l, back=back, out=out, own=own, g=g, f=f):
                pltpu.make_async_remote_copy(
                    src_ref=back.at[l], dst_ref=out.at[own], send_sem=back_send.at[g], recv_sem=back_recv.at[f], device_id={"lon": l}, device_id_type=MESH
                ).start()

        @pl.when(source)
        def _(back=back, out=out, own=own, f=f):
            pltpu.make_async_copy(back.at[me], out.at[own], back_recv.at[f]).start()

        @pl.when(jnp.logical_not(source))
        def _(out=out, g=g, f=f):
            if g == 0:
                blank[...] = jnp.zeros_like(blank)
            if g < 2:
                pltpu.make_async_copy(blank, out, back_recv.at[f]).start()

    ocean_copy.wait()

    @pl.when(source)
    def _():
        for g, (field, first, depth, got, back, out, f) in enumerate(groups):
            sent = field.at[pl.ds(0, depth * (n_lon - 1))]
            pltpu.make_async_copy(sent, sent, fwd_send.at[g]).wait()
        told = note.at[pl.ds(0, NBLK - 1)]
        pltpu.make_async_copy(told, told, note_send).wait()

    @pl.when(jnp.logical_not(source))
    def _():
        pltpu.make_async_copy(note, note, note_send).wait()

    for g, (field, first, depth, got, back, out, f) in enumerate(groups):

        @pl.when(source)
        def _(back=back, g=g):
            sent = back.at[pl.ds(0, NBLK - 1)]
            pltpu.make_async_copy(sent, sent, back_send.at[g]).wait()

        @pl.when(jnp.logical_not(source))
        def _(back=back, g=g):
            pltpu.make_async_copy(back, back, back_send.at[g]).wait()

    for f, out in enumerate((out_v, out_u)):
        pltpu.make_async_copy(out, out, back_recv.at[f]).wait()


def finish_kernel(ocean_in, u_in, v_in, ocean_out, u_out, v_out, sems):
    pairs = ((ocean_in, ocean_out), (u_in, u_out), (v_in, v_out))
    copies = [pltpu.make_async_copy(here, there, sems.at[i]) for i, (here, there) in enumerate(pairs)]
    for copy in copies:
        copy.start()
    for copy in copies:
        copy.wait()


def per_device(
    ocean_adjoint,
    mixing_coef,
    land_mask,
    remap_src,
    remap_dst,
    remap_live,
    remap_weight,
    atm_u,
    atm_v,
    spectral_nu,
    band_points,
):
    lon_devices = lax.axis_size("lon")
    levels = ocean_adjoint.shape[0]
    slots = remap_src.shape[2:]
    tile = ocean_adjoint.shape[1:]
    m = 16 * NBLK
    f32, bf16, dma = jnp.float32, jnp.bfloat16, pltpu.SemaphoreType.DMA
    smem = pl.BlockSpec(memory_space=pltpu.SMEM)
    hbm = pl.BlockSpec(memory_space=pltpu.HBM)
    anywhere = pl.BlockSpec(memory_space=pl.ANY)
    one = (1,) + atm_u.shape[1:]
    two = (2,) + atm_u.shape[1:]
    edge = (levels + 8, BLK)
    shapes = (
        jax.ShapeDtypeStruct(ocean_adjoint.shape, f32),
        jax.ShapeDtypeStruct(atm_u.shape, bf16),
        jax.ShapeDtypeStruct(atm_v.shape, bf16),
    )
    results = pl.pallas_call(
        window_kernel,
        out_shape=tuple(pltpu.VMEM(x.shape, x.dtype) for x in shapes),
        in_specs=[smem] + [hbm] * 10,
        out_specs=(anywhere, anywhere, anywhere),
        scratch_shapes=[
            pltpu.SMEM(spectral_nu.shape, f32),
            pltpu.SMEM(slots[::-1], jnp.int32),
            pltpu.SMEM(slots[::-1], jnp.int32),
            pltpu.SMEM(slots[::-1], jnp.int32),
            pltpu.VMEM(ocean_adjoint.shape, f32),
            pltpu.VMEM(mixing_coef.shape, f32),
            pltpu.VMEM(land_mask.shape, jnp.int32),
            pltpu.VMEM((NBLK, slots[1], BLK, BLK), bf16),
            pltpu.VMEM(one, bf16),
            dma((9,)),
            pltpu.VMEM((levels + 1,) + tile, f32),
            pltpu.VMEM((levels,) + tile, f32),
            pltpu.VMEM((levels,) + tile, f32),
            pltpu.VMEM(edge, f32),
            pltpu.VMEM(edge, f32),
            pltpu.VMEM(tile, f32),
            pltpu.VMEM(tile, f32),
            pltpu.VMEM(edge, f32),
            pltpu.VMEM(edge, f32),
            pltpu.VMEM(tile, f32),
            pltpu.VMEM(tile, f32),
            dma((4,)),
            dma((4,)),
            pltpu.VMEM(tile, f32),
            pltpu.VMEM((NBLK, 4, BLK), f32),
            pltpu.VMEM((lon_devices, 4, BLK), f32),
            dma,
            dma,
            pltpu.VMEM(one, bf16),
            pltpu.VMEM((NBLK,) + two, bf16),
            pltpu.VMEM((NBLK,) + one, bf16),
            pltpu.VMEM((NBLK,) + one, bf16),
            dma((3,)),
            dma((3,)),
            pltpu.VMEM((2, 16, K), f32),
            pltpu.VMEM((2, 16, K), f32),
            pltpu.VMEM((2, K // 16, SEGLON), f32),
            pltpu.VMEM((2, 16, SEGLON), f32),
            pltpu.VMEM((SEGLON, 2 * K), bf16),
            pltpu.VMEM((2 * K, SEGLON), bf16),
            pltpu.VMEM((2, TWROWS, K), f32),
            pltpu.VMEM((m, SEGLON), bf16),
            pltpu.VMEM((K // KT, 2, m, KT), f32),
            pltpu.VMEM((m, 2 * K), bf16),
            pltpu.VMEM((m, SEGLON), f32),
            pltpu.VMEM((NBLK,) + two, bf16),
            pltpu.VMEM((NBLK,) + one, bf16),
            pltpu.VMEM((NBLK,) + one, bf16),
            pltpu.VMEM(atm_u.shape, bf16),
            dma((3,)),
            dma((2,)),
            dma,
        ],
        compiler_params=pltpu.CompilerParams(collective_id=0, has_side_effects=True),
        name="window",
    )(
        band_points,
        spectral_nu,
        remap_src.reshape(slots).T,
        remap_dst.reshape(slots).T,
        remap_live.reshape(slots).T,
        ocean_adjoint,
        mixing_coef,
        land_mask,
        remap_weight.reshape(remap_weight.shape[2:]),
        atm_u,
        atm_v,
    )
    return pl.pallas_call(
        finish_kernel,
        out_shape=shapes,
        in_specs=[pl.BlockSpec(memory_space=pltpu.VMEM)] * 3,
        out_specs=(hbm, hbm, hbm),
        scratch_shapes=[dma((3,))],
        compiler_params=pltpu.CompilerParams(vmem_limit_bytes=8 << 20),
        name="finish",
    )(*results)


def solution(mesh):
    placed = (
        P(None, "ocn", "lon"),
        P(None, "ocn", "lon"),
        P("ocn", "lon"),
        P("ocn", "lon", None, None),
        P("ocn", "lon", None, None),
        P("ocn", "lon", None, None),
        P("ocn", "lon", None, None, None, None),
        P(None, "ocn", "lon"),
        P(None, "ocn", "lon"),
        P(),
        P("ocn"),
    )
    return jax.shard_map(
        per_device,
        mesh=mesh,
        in_specs=placed,
        out_specs=(P(None, "ocn", "lon"), P(None, "ocn", "lon"), P(None, "ocn", "lon")),
        check_vma=False,
    )
```

```python
import math

import jax
import jax.numpy as jnp
from jax import lax
from jax.experimental import pallas as pl
from jax.experimental.pallas import tpu as pltpu
from jax.sharding import PartitionSpec as P

K = 1280
BLK = 128
SEGLON = 256
NBLK = 21
TWROWS = 24
KT = 256
NU_MIX = 0.2
MESH = pl.DeviceIdType.MESH

COS_C = [(-1.0) ** m * (2.0 * math.pi) ** (2 * m) / math.factorial(2 * m) for m in range(11)]
SIN_C = [(-1.0) ** m * (2.0 * math.pi) ** (2 * m + 1) / math.factorial(2 * m + 1) for m in range(11)]


def iota(shape, dim):
    return lax.broadcasted_iota(jnp.int32, shape, dim).astype(jnp.float32)


def cos_sin(steps, points):
    inverse = 1.0 / points
    turns = jnp.floor(steps * inverse + 0.5)
    part = (steps - turns * points) * inverse
    square = part * part
    cosine = jnp.full_like(square, COS_C[10])
    sine = jnp.full_like(square, SIN_C[10])
    for m in range(9, -1, -1):
        cosine = cosine * square + COS_C[m]
        sine = sine * square + SIN_C[m]
    return cosine, sine * part


def build_tables(points, coarse, fine, coarse_t, fine_t, table, table_t, twiddle):
    n_row = jnp.full((16, K), points, jnp.float32)
    step_row, wave_row = iota((16, K), 0), iota((16, K), 1)
    coarse[0], coarse[1] = cos_sin(16.0 * step_row * wave_row, n_row)
    fine[0], fine[1] = cos_sin(step_row * wave_row, n_row)
    n_tw = jnp.full((TWROWS, K), points, jnp.float32)
    twiddle[0], twiddle[1] = cos_sin(float(SEGLON) * iota((TWROWS, K), 0) * iota((TWROWS, K), 1), n_tw)
    n_t = jnp.full((K // 16, SEGLON), points, jnp.float32)
    coarse_t[0], coarse_t[1] = cos_sin(16.0 * iota((K // 16, SEGLON), 0) * iota((K // 16, SEGLON), 1), n_t)
    n_f = jnp.full((16, SEGLON), points, jnp.float32)
    fine_t[0], fine_t[1] = cos_sin(iota((16, SEGLON), 0) * iota((16, SEGLON), 1), n_f)

    def rows(p, carry):
        cos_p, sin_p = coarse[0, pl.ds(p, 1), :], coarse[1, pl.ds(p, 1), :]
        here = pl.ds(pl.multiple_of(16 * p, 16), 16)
        table[here, 0:K] = (cos_p * fine[0] - sin_p * fine[1]).astype(jnp.bfloat16)
        table[here, K : 2 * K] = (sin_p * fine[0] + cos_p * fine[1]).astype(jnp.bfloat16)
        return carry

    lax.fori_loop(0, SEGLON // 16, rows, 0)

    def rows_t(p, carry):
        cos_p, sin_p = coarse_t[0, pl.ds(p, 1), :], coarse_t[1, pl.ds(p, 1), :]
        here = pl.ds(pl.multiple_of(16 * p, 16), 16)
        table_t[here, :] = (cos_p * fine_t[0] - sin_p * fine_t[1]).astype(jnp.bfloat16)
        table_t[pl.ds(pl.multiple_of(K + 16 * p, 16), 16), :] = (sin_p * fine_t[0] + cos_p * fine_t[1]).astype(jnp.bfloat16)
        return carry

    lax.fori_loop(0, K // 16, rows_t, 0, unroll=2)


def spectral(rows, points, viscosity, packed, table, table_t, twiddle, raw, spread, result):
    total = NBLK * rows
    half = (total // 2 + 15) // 16 * 16
    scale = 2.0 / jnp.full((rows, KT), points, jnp.float32)

    def transform(t):
        for part in range(2):
            at = part * K + t * KT
            raw[t, part, 0:total, :] = jnp.dot(packed[0:total, :], table[:, at : at + KT], preferred_element_type=jnp.float32)

    def twist(t):
        cos_at, sin_at = slice(t * KT, (t + 1) * KT), slice(K + t * KT, K + (t + 1) * KT)
        sum_c = jnp.zeros((rows, KT), jnp.float32)
        sum_s = jnp.zeros((rows, KT), jnp.float32)
        for l in range(NBLK):
            here = slice(l * rows, (l + 1) * rows)
            part_c, part_s = raw[t, 0, here, :], raw[t, 1, here, :]
            tw_c, tw_s = twiddle[0, l : l + 1, cos_at], twiddle[1, l : l + 1, cos_at]
            sum_c += tw_c * part_c - tw_s * part_s
            sum_s += tw_s * part_c + tw_c * part_s
        ratio = (iota((rows, KT), 1) + float(t * KT)) * (1.0 / K)
        damping = scale / (1.0 + viscosity * ratio * ratio)
        sum_c *= damping
        sum_s *= damping
        for l in range(NBLK):
            here = slice(l * rows, (l + 1) * rows)
            tw_c, tw_s = twiddle[0, l : l + 1, cos_at], twiddle[1, l : l + 1, cos_at]
            spread[here, cos_at] = (tw_c * sum_c + tw_s * sum_s).astype(jnp.bfloat16)
            spread[here, sin_at] = (tw_c * sum_s - tw_s * sum_c).astype(jnp.bfloat16)

    transform(0)
    for t in range(K // KT):
        if t + 1 < K // KT:
            transform(t + 1)
        twist(t)
    for here in (slice(0, half), slice(half, total)):
        result[here] = jnp.dot(spread[here], table_t[...], preferred_element_type=jnp.float32)


STEPS = [((2, 1, 3, 0)[(a + b) % 4], (2, 1, 3, 0)[b], core) for a in range(4) for b in range(4) for core in range(2)]


def wrapped(index, count):
    return jnp.where(index >= count, index - count, index)


def shift_rows(cells, down, edge):
    row = lax.broadcasted_iota(jnp.int32, cells.shape, 0)
    last = cells.shape[0] - 1
    if down:
        return jnp.where(row == 0, edge, pltpu.roll(cells, 1, 0))
    return jnp.where(row == last, edge, pltpu.roll(cells, last, 0))


def shift_cols(cells, right, edge):
    lane = lax.broadcasted_iota(jnp.int32, cells.shape, 1)
    last = cells.shape[1] - 1
    if right:
        return jnp.where(lane == 0, edge, pltpu.roll(cells, 1, 1))
    return jnp.where(lane == last, edge, pltpu.roll(cells, last, 1))


def window_kernel(
    n_ref, nu_hbm, src_hbm, dst_hbm, live_hbm, force_hbm, mix_hbm, mask_hbm, weight_hbm, u_hbm, v_hbm,
    out_ocean, out_u, out_v,
    nu_ref, src_ref, dst_ref, live_ref, force, mix, mask, weight, last_u, load_sem,
    cells, ratio, ocean, send_n, send_s, send_w, send_e, got_n, got_s, got_w, got_e, halo_send, halo_recv,
    flux, note, notes, note_send, note_recv,
    stage, got_v, got_even, got_odd, fwd_send, fwd_recv,
    coarse, fine, coarse_t, fine_t, table, table_t, twiddle,
    packed, raw, spread, result, back_v, back_even, back_odd, blank, back_send, back_recv, ocean_sem,
):
    me, oc = lax.axis_index("lon"), lax.axis_index("ocn")
    n_lon, n_ocn = lax.axis_size("lon"), lax.axis_size("ocn")
    levels = cells.shape[0] - 1
    last_owner = n_lon - 1
    share = 2
    source = me < NBLK
    start_at = wrapped(me, NBLK)
    x, y, core = me // 8, lax.rem(me // 2, 4), lax.rem(me, 2)
    x_at = [8 * wrapped(x + d, 4) for d in range(4)]
    y_at = [2 * wrapped(y + d, 4) for d in range(4)]
    c_at = [core, 1 - core]

    def peer(step):
        return x_at[step[0]] + y_at[step[1]] + c_at[step[2]]


    def mine(t):
        return pl.ds(share * t, share)

    loads = [
        pltpu.make_async_copy(force_hbm, force, load_sem.at[0]),
        pltpu.make_async_copy(mix_hbm, mix, load_sem.at[1]),
        pltpu.make_async_copy(mask_hbm, mask, load_sem.at[2]),
        pltpu.make_async_copy(weight_hbm.at[pl.ds(0, NBLK)], weight, load_sem.at[3]),
        pltpu.make_async_copy(u_hbm.at[pl.ds(share * n_lon - 1, 1)], last_u, load_sem.at[4]),
        pltpu.make_async_copy(nu_hbm, nu_ref, load_sem.at[5]),
        pltpu.make_async_copy(src_hbm, src_ref, load_sem.at[6]),
        pltpu.make_async_copy(dst_hbm, dst_ref, load_sem.at[7]),
        pltpu.make_async_copy(live_hbm, live_ref, load_sem.at[8]),
    ]
    barrier = pltpu.get_barrier_semaphore()
    for step in STEPS:
        if step != (0, 0, 0):
            pl.semaphore_signal(barrier, inc=1, device_id={"lon": peer(step)}, device_id_type=MESH)

    @pl.when(oc > 0)
    def _():
        pl.semaphore_signal(barrier, inc=1, device_id={"ocn": oc - 1}, device_id_type=MESH)

    @pl.when(oc < n_ocn - 1)
    def _():
        pl.semaphore_signal(barrier, inc=1, device_id={"ocn": oc + 1}, device_id_type=MESH)

    for load in loads:
        load.start()

    for load in loads[:3]:
        load.wait()
    zero = jnp.zeros(force.shape[1:], jnp.float32)
    rat, val, below = zero, zero, zero
    for z in range(levels - 1, -1, -1):
        above = mix[z - 1] if z > 0 else zero
        inv = 1.0 / (1.0 + above + below * (1.0 - rat))
        val = (force[z] + below * val) * inv
        rat = above * inv
        cells[z] = val
        ratio[z] = rat
        below = above
    lane = lax.broadcasted_iota(jnp.int32, zero.shape, 1)
    west, east = zero, zero
    send_n[pl.ds(levels, 8), :] = zero
    send_s[pl.ds(levels, 8), :] = zero
    s = zero
    for z in range(levels + 1):
        if z < levels:
            s = cells[z] + ratio[z] * s if z > 0 else cells[0]
        else:
            s = mask[...].astype(jnp.float32)
        cells[z] = s
        send_n[z : z + 1, :] = s[0:1, :]
        send_s[z : z + 1, :] = s[7:8, :]
        west = jnp.where(lane == z, jnp.broadcast_to(s[:, 0:1], s.shape), west)
        east = jnp.where(lane == z, jnp.broadcast_to(s[:, BLK - 1 : BLK], s.shape), east)
    send_w[...] = west
    send_e[...] = east

    pl.semaphore_wait(barrier, n_lon - 1 + (oc > 0).astype(jnp.int32) + (oc < n_ocn - 1).astype(jnp.int32))

    sides = (
        (oc > 0, oc < n_ocn - 1, {"ocn": oc - 1}, send_n, got_s),
        (oc < n_ocn - 1, oc > 0, {"ocn": oc + 1}, send_s, got_n),
        (me > 0, me < n_lon - 1, {"lon": me - 1}, send_w, got_e),
        (me < n_lon - 1, me > 0, {"lon": me + 1}, send_e, got_w),
    )

    def halo(i):
        has, gets, where, out, into = sides[i]
        return has, gets, into, pltpu.make_async_remote_copy(
            src_ref=out, dst_ref=into, send_sem=halo_send.at[i], recv_sem=halo_recv.at[i], device_id=where, device_id_type=MESH
        )

    for i in range(4):
        has, gets, into, copy = halo(i)
        pl.when(has)(copy.start)

        @pl.when(jnp.logical_not(gets))
        def _(into=into):
            into[...] = jnp.zeros_like(into)

    groups = (
        (v_hbm, 0, 2, got_v, back_v, out_v, 0),
        (u_hbm, 0, 1, got_even, back_even, out_u, 1),
        (u_hbm, 1, 1, got_odd, back_odd, out_u, 1),
    )

    def send_rows(g):
        field, first, depth, got = groups[g][:4]

        def rows_of(t):
            return field.at[pl.ds(share * t + first, depth)]

        for step in STEPS:
            if step == (0, 0, 0):
                continue
            t = peer(step)
            copy = pltpu.make_async_remote_copy(
                src_ref=rows_of(t), dst_ref=got.at[me], send_sem=fwd_send.at[g], recv_sem=fwd_recv.at[g], device_id={"lon": t}, device_id_type=MESH
            )
            if g < 2:
                copy.start()
            else:
                pl.when(t != last_owner)(copy.start)

        pltpu.make_async_copy(rows_of(me), got.at[me], fwd_recv.at[g]).start()

    @pl.when(source)
    def _():
        for g in range(2):
            send_rows(g)

    points = n_ref[0].astype(jnp.float32)
    build_tables(points, coarse, fine, coarse_t, fine_t, table, table_t, twiddle)

    for i in range(4):
        has, gets, into, copy = halo(i)
        pl.when(gets)(copy.wait_recv)
        pl.when(has)(copy.wait_send)

    m = cells[levels]
    m_n, m_s = shift_rows(m, True, got_n[levels : levels + 1, :]), shift_rows(m, False, got_s[levels : levels + 1, :])
    m_w = shift_cols(m, True, jnp.broadcast_to(got_w[:, levels : levels + 1], m.shape))
    m_e = shift_cols(m, False, jnp.broadcast_to(got_e[:, levels : levels + 1], m.shape))

    def mixed(z):
        s = cells[z]
        near = m_n * (shift_rows(s, True, got_n[z : z + 1, :]) - s)
        near += m_s * (shift_rows(s, False, got_s[z : z + 1, :]) - s)
        near += m_w * (shift_cols(s, True, jnp.broadcast_to(got_w[:, z : z + 1], s.shape)) - s)
        near += m_e * (shift_cols(s, False, jnp.broadcast_to(got_e[:, z : z + 1], s.shape)) - s)
        return m * (s + NU_MIX * near)

    surface = mixed(0)
    ocean[0] = surface
    flux[...] = surface.astype(jnp.bfloat16).astype(jnp.float32)
    for load in loads[3:4] + loads[6:]:
        load.wait()

    def owner(p, carry):
        one = flux[pl.ds(src_ref[0, p], 1), :]
        two = flux[pl.ds(src_ref[1, p], 1), :]
        row = lax.broadcasted_iota(jnp.int32, (8, BLK), 0)
        lhs = jnp.concatenate([jnp.where(row == 0, one, 0.0), jnp.where(row == 1, two, 0.0)], 1).astype(jnp.bfloat16)
        both = jnp.concatenate([weight[p, 0], weight[p, 1]], 1)
        got = lax.dot_general(lhs, both, (((1,), (1,)), ((), ())), preferred_element_type=jnp.float32)
        code_0 = live_ref[0, p] * (dst_ref[0, p] + 1) - 1
        code_1 = live_ref[1, p] * (dst_ref[1, p] + 1) - 1
        codes = jnp.where(row == 2, code_0, code_1).astype(jnp.float32)
        note[p] = jnp.where(row < 2, got, codes)[0:4]
        return carry

    lax.fori_loop(0, NBLK, owner, 0, unroll=21)

    for step in STEPS:
        if step == (0, 0, 0):
            continue
        p = peer(step)

        @pl.when(p < NBLK)
        def _(p=p):
            pltpu.make_async_remote_copy(
                src_ref=note.at[p], dst_ref=notes.at[me], send_sem=note_send, recv_sem=note_recv, device_id={"lon": p}, device_id_type=MESH
            ).start()

    @pl.when(source)
    def _():
        pltpu.make_async_copy(note.at[me], notes.at[me], note_recv).start()
        send_rows(2)

    for z in range(1, levels):
        ocean[z] = mixed(z)
    ocean_copy = pltpu.make_async_copy(ocean, out_ocean, ocean_sem)
    ocean_copy.start()
    loads[4].wait()

    def couple():
        pltpu.make_async_copy(notes, notes, note_recv).wait()
        even = 2.0 * iota((8, BLK), 0)
        odd = even + 1.0

        def add(l, sums):
            sum_even, sum_odd = sums
            block = notes[l]
            for c in range(2):
                value, code = block[c : c + 1, :], block[c + 2 : c + 3, :]
                sum_even += jnp.where(code == even, value, 0.0)
                sum_odd += jnp.where(code == odd, value, 0.0)
            return sum_even, sum_odd

        blank_sum = jnp.zeros((8, BLK), jnp.float32)
        sum_even, sum_odd = lax.fori_loop(0, n_lon, add, (blank_sum, blank_sum), unroll=4)
        coupling = jnp.concatenate([sum_even, sum_odd], 1)
        stage[0] = (last_u[0].astype(jnp.float32) + coupling).astype(jnp.bfloat16)
        pltpu.make_async_remote_copy(
            src_ref=stage, dst_ref=got_odd.at[me], send_sem=fwd_send.at[2], recv_sem=fwd_recv.at[2], device_id={"lon": last_owner}, device_id_type=MESH
        ).start()

    loads[5].wait()
    for g, (field, first, depth, got, back, out, f) in enumerate(groups):
        rows = 8 * depth
        column = iota((rows, SEGLON), 1)
        if g == 1:
            pl.when(source)(couple)
        pltpu.make_async_copy(got, got, fwd_recv.at[g]).wait()

        def pack(l, carry, got=got, rows=rows, column=column):
            inside = column + (l * SEGLON).astype(jnp.float32) < points
            block = got[l].astype(jnp.float32).reshape(rows, SEGLON)
            result[pl.ds(pl.multiple_of(rows * l, 8), rows), :] = jnp.where(inside, block, 0.0)
            return carry

        lax.fori_loop(0, NBLK, pack, 0, unroll=3)
        total = pl.ds(0, NBLK * rows)
        packed[total, :] = result[total, :].astype(jnp.bfloat16)
        viscosity = nu_ref[share * me + first]
        if depth == 2:
            viscosity = jnp.where(lax.broadcasted_iota(jnp.int32, (rows, KT), 0) < 8, viscosity, nu_ref[share * me + 1])
        spectral(rows, points, viscosity, packed, table, table_t, twiddle, raw, spread, result)
        own = pl.ds(share * me + first, depth)

        def unpack(l, carry, back=back, rows=rows, depth=depth, column=column):
            inside = column + (l * SEGLON).astype(jnp.float32) < points
            block = result[pl.ds(pl.multiple_of(rows * l, 8), rows), :]
            back[l] = jnp.where(inside, block, 0.0).reshape(depth, 8, SEGLON).astype(jnp.bfloat16)
            return carry

        lax.fori_loop(0, NBLK, unpack, 0, unroll=7)
        for step in STEPS:
            if step == (0, 0, 0):
                continue
            l = peer(step)

            @pl.when(l < NBLK)
            def _(l=l, back=back, out=out, own=own, g=g, f=f):
                pltpu.make_async_remote_copy(
                    src_ref=back.at[l], dst_ref=out.at[own], send_sem=back_send.at[g], recv_sem=back_recv.at[f], device_id={"lon": l}, device_id_type=MESH
                ).start()

        @pl.when(source)
        def _(back=back, out=out, own=own, f=f):
            pltpu.make_async_copy(back.at[me], out.at[own], back_recv.at[f]).start()

        @pl.when(jnp.logical_not(source))
        def _(out=out, g=g, f=f):
            if g == 0:
                blank[...] = jnp.zeros_like(blank)
            if g < 2:
                pltpu.make_async_copy(blank, out, back_recv.at[f]).start()

    ocean_copy.wait()

    @pl.when(source)
    def _():
        for g, (field, first, depth, got, back, out, f) in enumerate(groups):
            sent = field.at[pl.ds(0, depth * (n_lon - 1))]
            pltpu.make_async_copy(sent, sent, fwd_send.at[g]).wait()
        told = note.at[pl.ds(0, NBLK - 1)]
        pltpu.make_async_copy(told, told, note_send).wait()

    @pl.when(jnp.logical_not(source))
    def _():
        pltpu.make_async_copy(note, note, note_send).wait()

    for g, (field, first, depth, got, back, out, f) in enumerate(groups):

        @pl.when(source)
        def _(back=back, g=g):
            sent = back.at[pl.ds(0, NBLK - 1)]
            pltpu.make_async_copy(sent, sent, back_send.at[g]).wait()

        @pl.when(jnp.logical_not(source))
        def _(back=back, g=g):
            pltpu.make_async_copy(back, back, back_send.at[g]).wait()

    for f, out in enumerate((out_v, out_u)):
        pltpu.make_async_copy(out, out, back_recv.at[f]).wait()


def finish_kernel(ocean_in, u_in, v_in, ocean_out, u_out, v_out, sems):
    pairs = ((ocean_in, ocean_out), (u_in, u_out), (v_in, v_out))
    copies = [pltpu.make_async_copy(here, there, sems.at[i]) for i, (here, there) in enumerate(pairs)]
    for copy in copies:
        copy.start()
    for copy in copies:
        copy.wait()


def per_device(
    ocean_adjoint,
    mixing_coef,
    land_mask,
    remap_src,
    remap_dst,
    remap_live,
    remap_weight,
    atm_u,
    atm_v,
    spectral_nu,
    band_points,
):
    lon_devices = lax.axis_size("lon")
    levels = ocean_adjoint.shape[0]
    slots = remap_src.shape[2:]
    tile = ocean_adjoint.shape[1:]
    m = 16 * NBLK
    f32, bf16, dma = jnp.float32, jnp.bfloat16, pltpu.SemaphoreType.DMA
    smem = pl.BlockSpec(memory_space=pltpu.SMEM)
    hbm = pl.BlockSpec(memory_space=pltpu.HBM)
    anywhere = pl.BlockSpec(memory_space=pl.ANY)
    one = (1,) + atm_u.shape[1:]
    two = (2,) + atm_u.shape[1:]
    edge = (levels + 8, BLK)
    shapes = (
        jax.ShapeDtypeStruct(ocean_adjoint.shape, f32),
        jax.ShapeDtypeStruct(atm_u.shape, bf16),
        jax.ShapeDtypeStruct(atm_v.shape, bf16),
    )
    results = pl.pallas_call(
        window_kernel,
        out_shape=tuple(pltpu.VMEM(x.shape, x.dtype) for x in shapes),
        in_specs=[smem] + [hbm] * 10,
        out_specs=(anywhere, anywhere, anywhere),
        scratch_shapes=[
            pltpu.SMEM(spectral_nu.shape, f32),
            pltpu.SMEM(slots[::-1], jnp.int32),
            pltpu.SMEM(slots[::-1], jnp.int32),
            pltpu.SMEM(slots[::-1], jnp.int32),
            pltpu.VMEM(ocean_adjoint.shape, f32),
            pltpu.VMEM(mixing_coef.shape, f32),
            pltpu.VMEM(land_mask.shape, jnp.int32),
            pltpu.VMEM((NBLK, slots[1], BLK, BLK), bf16),
            pltpu.VMEM(one, bf16),
            dma((9,)),
            pltpu.VMEM((levels + 1,) + tile, f32),
            pltpu.VMEM((levels,) + tile, f32),
            pltpu.VMEM((levels,) + tile, f32),
            pltpu.VMEM(edge, f32),
            pltpu.VMEM(edge, f32),
            pltpu.VMEM(tile, f32),
            pltpu.VMEM(tile, f32),
            pltpu.VMEM(edge, f32),
            pltpu.VMEM(edge, f32),
            pltpu.VMEM(tile, f32),
            pltpu.VMEM(tile, f32),
            dma((4,)),
            dma((4,)),
            pltpu.VMEM(tile, f32),
            pltpu.VMEM((NBLK, 4, BLK), f32),
            pltpu.VMEM((lon_devices, 4, BLK), f32),
            dma,
            dma,
            pltpu.VMEM(one, bf16),
            pltpu.VMEM((NBLK,) + two, bf16),
            pltpu.VMEM((NBLK,) + one, bf16),
            pltpu.VMEM((NBLK,) + one, bf16),
            dma((3,)),
            dma((3,)),
            pltpu.VMEM((2, 16, K), f32),
            pltpu.VMEM((2, 16, K), f32),
            pltpu.VMEM((2, K // 16, SEGLON), f32),
            pltpu.VMEM((2, 16, SEGLON), f32),
            pltpu.VMEM((SEGLON, 2 * K), bf16),
            pltpu.VMEM((2 * K, SEGLON), bf16),
            pltpu.VMEM((2, TWROWS, K), f32),
            pltpu.VMEM((m, SEGLON), bf16),
            pltpu.VMEM((K // KT, 2, m, KT), f32),
            pltpu.VMEM((m, 2 * K), bf16),
            pltpu.VMEM((m, SEGLON), f32),
            pltpu.VMEM((NBLK,) + two, bf16),
            pltpu.VMEM((NBLK,) + one, bf16),
            pltpu.VMEM((NBLK,) + one, bf16),
            pltpu.VMEM(atm_u.shape, bf16),
            dma((3,)),
            dma((2,)),
            dma,
        ],
        compiler_params=pltpu.CompilerParams(collective_id=0, has_side_effects=True),
        name="window",
    )(
        band_points,
        spectral_nu,
        remap_src.reshape(slots).T,
        remap_dst.reshape(slots).T,
        remap_live.reshape(slots).T,
        ocean_adjoint,
        mixing_coef,
        land_mask,
        remap_weight.reshape(remap_weight.shape[2:]),
        atm_u,
        atm_v,
    )
    return pl.pallas_call(
        finish_kernel,
        out_shape=shapes,
        in_specs=[pl.BlockSpec(memory_space=pltpu.VMEM)] * 3,
        out_specs=(hbm, hbm, hbm),
        scratch_shapes=[dma((3,))],
        compiler_params=pltpu.CompilerParams(vmem_limit_bytes=8 << 20),
        name="finish",
    )(*results)


def solution(mesh):
    placed = (
        P(None, "ocn", "lon"),
        P(None, "ocn", "lon"),
        P("ocn", "lon"),
        P("ocn", "lon", None, None),
        P("ocn", "lon", None, None),
        P("ocn", "lon", None, None),
        P("ocn", "lon", None, None, None, None),
        P(None, "ocn", "lon"),
        P(None, "ocn", "lon"),
        P(),
        P("ocn"),
    )
    return jax.shard_map(
        per_device,
        mesh=mesh,
        in_specs=placed,
        out_specs=(P(None, "ocn", "lon"), P(None, "ocn", "lon"), P(None, "ocn", "lon")),
        check_vma=False,
    )
```
